512 devices in a mesh: depth: 16 (over z), lat: 32 (over x, y, core).
Axes of the slice: x: 4, y: 4, z: 16, core: 2. Of those that a mesh axis runs over, the one named last changes fastest.
Arguments:
- volume: float32 [4, 64, 512, 512], P(None, 'depth', 'lat'), may hold values from 0 to 2
- offsets: int32 [8, 64], P(None, 'depth'), may hold values from -4 to 4, as said below
- view_ids: int32 [2], replicated, may hold values from 0 to 7
- weights: float32 [2, 4, 512, 512], P(None, None, 'lat'), may hold values from -6 to 6
Outputs:
- image_out: float32 [2, 4, 512, 512], P(None, None, 'lat')
- grad_out: float32 [4, 64, 512, 512], P(None, 'depth', 'lat')
The draws below stay inside these ranges and needn't reach their ends.
Inputs may be any that keep to these rules, and one draw needn't show every extreme that they name: `offsets`: in every pose some slice has offset 4 and another has offset -4.
All inputs are finite; a program needn't handle non-finite values.
Results may differ from the reference program's by a relative error of at most 0.00017.
Values sent between devices are 32-bit elements; how exact they have to be, the bound alone decides.
No kernel may reach another device: no remote copies, remote signals or barrier semaphores. Data moves between devices by JAX's collectives and lax.ppermute only.
A program may use at most 64 MiB of HBM per device.

```python
import jax
import jax.numpy as jnp
from jax import lax

NX = 512
HALO = 4
VIEWS = 2
POSES = 8
NZ = 64
NY = 512


def draw_offsets(key, part):
    key_base = jax.random.fold_in(key, 11)
    key_high = jax.random.fold_in(key, 12)
    key_step = jax.random.fold_in(key, 13)
    base = jax.random.randint(key_base, (POSES, NZ), -HALO, HALO + 1)
    high_pos = jax.random.randint(key_high, (POSES, 1), 0, NZ)
    low_pos = (high_pos + 1 + jax.random.randint(key_step, (POSES, 1), 0, NZ - 1)) % NZ
    column = jnp.arange(NZ)[None, :]
    base = jnp.where(column == high_pos, HALO, base)
    base = jnp.where(column == low_pos, -HALO, base)
    return base.astype(jnp.int32)


def level_of(own_key, dims, cuts, low, top_value):
    def one(position, parts):
        draws = jax.random.uniform(jax.random.fold_in(jax.random.fold_in(own_key, 6), position), (parts,), jnp.float32, low / len(cuts), top_value / len(cuts))
        return jnp.repeat(jnp.exp(draws), dims[position] // parts).reshape((-1,) + (1,) * (len(dims) - position - 1))

    gain = one(*cuts[0])
    for cut in cuts[1:]:
        gain = gain * one(*cut)
    return gain


def centred(rng, shape, width, limit, pieces=(), held_as=jnp.bfloat16):
    drawn = jax.random.normal(rng, shape, jnp.float32) * width
    if len(pieces) > 0:
        drawn = level_of(rng, shape, pieces, -0.22, 0.18) * drawn
    return jnp.clip(drawn, min=-limit, max=limit).astype(held_as)


def setup_inputs(seed: int = 0) -> dict:
    streams_of = jax.random.split(jax.random.key(seed), 5)
    return {
        "volume": jnp.clip(2.0 * jax.random.uniform(streams_of[0], (4, NZ, NY, NX), jnp.float32) ** level_of(streams_of[0], (4, NZ, NY, NX), ((1, 16), (2, 32)), -0.2, 0.2), 0.0, 2.0),
        "offsets": draw_offsets(jax.random.fold_in(streams_of[4], 71), 0),
        "view_ids": jax.random.randint(streams_of[2], (VIEWS,), 0, POSES).astype(jnp.int32),
        "weights": centred(streams_of[3], (VIEWS, 4, NY, NX), 1.0, 6.0, ((2, 32),), jnp.float32),
    }


def reference(volume, offsets, view_ids, weights):
    depth_total = volume.shape[1]
    row_count = volume.shape[2]
    col_count = volume.shape[3]
    view_count = view_ids.shape[0]
    view_shift = offsets[view_ids]
    padded = jnp.pad(volume, ((0, 0), (0, 0), (HALO, HALO), (0, 0)))
    stacked = jnp.moveaxis(padded, 1, 0)
    shifts_k = jnp.transpose(view_shift)

    def sheared_of(layer, shift_pair):
        return jax.vmap(lambda offset_row: lax.dynamic_slice_in_dim(layer, HALO - offset_row, row_count, 1))(shift_pair)

    def front_step(carried, element):
        transmit, radiance = carried
        layer, shift_pair = element
        sheared = sheared_of(layer, shift_pair)
        alpha_k = 1.0 - jnp.exp(-sheared[:, 3] / depth_total)
        radiance = radiance + (transmit * alpha_k)[:, None] * sheared[:, :3]
        return (transmit * (1.0 - alpha_k), radiance), transmit

    begin = (jnp.ones((view_count, row_count, col_count), jnp.float32),
             jnp.zeros((view_count, 3, row_count, col_count), jnp.float32))
    (transmit, radiance), transmit_all = lax.scan(front_step, begin, (stacked, shifts_k))
    image_out = jnp.concatenate([radiance, (1.0 - transmit)[:, None]], axis=1)

    def back_step(behind, element):
        layer, shift_pair, transmit_k = element
        sheared = sheared_of(layer, shift_pair)
        alpha_k = 1.0 - jnp.exp(-sheared[:, 3] / depth_total)
        glow_term = jnp.sum(weights[:, :3] * sheared[:, :3], axis=1)
        grad_emit = depth_total * (transmit_k * alpha_k)[:, None] * weights[:, :3]
        grad_absorb = (1.0 - alpha_k) * transmit_k * (glow_term - behind)
        grad_img = jnp.concatenate([grad_emit, grad_absorb[:, None]], axis=1)
        grad_pad = jnp.pad(grad_img, ((0, 0), (0, 0), (HALO, HALO), (0, 0)))
        back_rows = jax.vmap(lambda plane_rows, offset_row: lax.dynamic_slice_in_dim(plane_rows, HALO + offset_row, row_count, 1))(grad_pad, shift_pair)
        behind = alpha_k * glow_term + (1.0 - alpha_k) * behind
        return behind, jnp.sum(back_rows, axis=0)

    unused, grad_all = lax.scan(back_step, -weights[:, 3], (stacked, shifts_k, transmit_all), reverse=True)
    grad_out = jnp.moveaxis(grad_all, 0, 1)
    return image_out, grad_out
```

```python
import jax
import jax.numpy as jnp
from jax import lax
from jax.experimental import pallas as pl
from jax.experimental.pallas import tpu as pltpu
from jax.sharding import PartitionSpec as P

HALO = 4
LANES = 128
VMEM = pl.BlockSpec(memory_space=pltpu.VMEM)
SMEM = pl.BlockSpec(memory_space=pltpu.SMEM)


def slab_kernel(
    depth_total, offs, vids, vol, low, high, w, agg, absorb_part, emit_part, ext
):
    channels, slabs, rows, cols = vol.shape
    views = w.shape[0]
    tiles = cols // LANES
    bands = rows // 8
    for c in range(channels):
        for k in range(slabs):
            for t in range(tiles):
                lanes = pl.ds(t * LANES, LANES)
                ext[c, k, t, 4:8, :] = low[c, k, :, lanes]
                ext[c, k, t, 8 : 8 + rows, :] = vol[c, k, :, lanes]
                ext[c, k, t, 8 + rows : 12 + rows, :] = high[c, k, :, lanes]
    for v in range(views):
        starts = [8 - offs[k, vids[v]] for k in range(slabs)]
        for t in range(tiles):
            lanes = pl.ds(t * LANES, LANES)
            weight = [w[v, c, :, lanes] for c in range(3)]
            transmit = jnp.ones((rows, LANES), jnp.float32)
            colour = [jnp.zeros((rows, LANES), jnp.float32) for _ in range(3)]
            alphas, keeps, glows, fronts = [], [], [], []
            for k in range(slabs):
                part = [ext[c, k, t, pl.ds(starts[k], rows), :] for c in range(channels)]
                keep = jnp.exp(part[3] * (-1.0 / depth_total))
                alpha = 1.0 - keep
                seen = transmit * alpha
                colour = [colour[c] + seen * part[c] for c in range(3)]
                emit_part[v, k, t] = seen * float(depth_total)
                glows.append(weight[0] * part[0] + weight[1] * part[1] + weight[2] * part[2])
                alphas.append(alpha)
                keeps.append(keep)
                transmit = transmit * keep
                fronts.append(transmit)
            behind = jnp.zeros((rows, LANES), jnp.float32)
            for k in range(slabs - 1, -1, -1):
                absorb_part[v, k, t] = fronts[k] * (glows[k] - behind)
                behind = alphas[k] * glows[k] + keeps[k] * behind
            for b in range(bands):
                owner = (v * bands + b) * tiles + t
                agg[owner, 0] = transmit[8 * b : 8 * b + 8]
                for c in range(3):
                    agg[owner, 1 + c] = colour[c][8 * b : 8 * b + 8]


def scan_kernel(place, agg, w, out):
    count = agg.shape[0]
    transmit = jnp.ones((8, LANES), jnp.float32)
    colour = [jnp.zeros((8, LANES), jnp.float32) for _ in range(3)]
    entering = []
    for s in range(count):
        entering.append(transmit)
        colour = [colour[c] + transmit * agg[s, 1 + c] for c in range(3)]
        transmit = transmit * agg[s, 0]
    opacity = 1.0 - transmit
    behind = -w[0, 3]
    for s in range(count - 1, -1, -1):
        passed = agg[s, 0] * behind
        out[s, 0] = entering[s]
        out[s, 1] = entering[s] * passed
        for c in range(3):
            out[s, 2 + c] = colour[c]
        out[s, 5] = opacity
        glow = w[0, 0] * agg[s, 1] + w[0, 1] * agg[s, 2] + w[0, 2] * agg[s, 3]
        behind = glow + passed


def grad_kernel(
    offs, vids, got, absorb_part, emit_part, w, main, low, high, image, shifted
):
    views, channels, rows, cols = w.shape
    slabs = main.shape[1]
    tiles = cols // LANES
    bands = rows // 8
    edge = jnp.zeros((8, LANES), jnp.float32)
    for v in range(views):
        for t in range(tiles):
            lanes = pl.ds(t * LANES, LANES)
            owners = [(v * bands + b) * tiles + t for b in range(bands)]
            front = jnp.concatenate([got[n, 0] for n in owners], axis=0)
            passed = jnp.concatenate([got[n, 1] for n in owners], axis=0)
            for b, n in enumerate(owners):
                for c in range(channels):
                    image[v, c, 8 * b : 8 * b + 8, lanes] = got[n, 2 + c]
            weight = [front * w[v, c, :, lanes] for c in range(3)]
            for k in range(slabs):
                emit = emit_part[v, k, t]
                parts = [emit * weight[c] for c in range(3)]
                parts.append(front * absorb_part[v, k, t] - passed)
                for c in range(channels):
                    shifted[v, k, c, t, 0:8, :] = edge
                    shifted[v, k, c, t, 8 : 8 + rows, :] = parts[c]
                    shifted[v, k, c, t, 8 + rows : 16 + rows, :] = edge
    for k in range(slabs):
        moves = [offs[k, vids[v]] for v in range(views)]
        for c in range(channels):
            for t in range(tiles):
                lanes = pl.ds(t * LANES, LANES)

                def total(start, size):
                    return sum(
                        shifted[v, k, c, t, pl.ds(start + moves[v], size), :]
                        for v in range(views)
                    )

                low[c, k, :, lanes] = total(4, 4)
                main[c, k, :, lanes] = total(8, rows)
                high[c, k, :, lanes] = total(8 + rows, 4)


def join_kernel(main, low, high, out):
    rows = main.shape[2]
    out[:, :, 0:4, :] = main[:, :, 0:4, :] + low[...]
    out[:, :, 4 : rows - 4, :] = main[:, :, 4 : rows - 4, :]
    out[:, :, rows - 4 :, :] = main[:, :, rows - 4 :, :] + high[...]


def on_device(volume, offsets, view_ids, weights):
    channels, slabs, rows, cols = volume.shape
    views = weights.shape[0]
    count = lax.axis_size("depth")
    strips = lax.axis_size("lat")
    tiles, bands = cols // LANES, rows // 8
    depth_total = slabs * count
    up = [(i, i + 1) for i in range(strips - 1)]
    down = [(i + 1, i) for i in range(strips - 1)]
    f32 = lambda *shape: jax.ShapeDtypeStruct(shape, jnp.float32)
    table = offsets.T

    low = lax.ppermute(volume[:, :, rows - HALO :], "lat", up)
    high = lax.ppermute(volume[:, :, :HALO], "lat", down)
    agg, absorb_part, emit_part = pl.pallas_call(
        lambda *refs: slab_kernel(depth_total, *refs),
        out_shape=(
            f32(count, 4, 8, LANES),
            f32(views, slabs, tiles, rows, LANES),
            f32(views, slabs, tiles, rows, LANES),
        ),
        in_specs=[SMEM, SMEM, VMEM, VMEM, VMEM, VMEM],
        out_specs=(VMEM, VMEM, VMEM),
        scratch_shapes=[pltpu.VMEM((channels, slabs, tiles, rows + 16, LANES), jnp.float32)],
        name="slab",
    )(table, view_ids, volume, low, high, weights)

    agg = lax.all_to_all(agg, "depth", 0, 0, tiled=True)
    place = lax.axis_index("depth").reshape(1).astype(jnp.int32)
    sent = pl.pallas_call(
        scan_kernel,
        out_shape=f32(count, 6, 8, LANES),
        grid_spec=pltpu.PrefetchScalarGridSpec(
            num_scalar_prefetch=1,
            grid=(1,),
            in_specs=[
                pl.BlockSpec((count, 4, 8, LANES), lambda i, z: (0, 0, 0, 0)),
                pl.BlockSpec(
                    (1, 4, 8, LANES),
                    lambda i, z: (z[0] // (bands * tiles), 0, (z[0] // tiles) % bands, z[0] % tiles),
                ),
            ],
            out_specs=pl.BlockSpec((count, 6, 8, LANES), lambda i, z: (0, 0, 0, 0)),
        ),
        name="scan",
    )(place, agg, weights)
    got = lax.all_to_all(sent, "depth", 0, 0, tiled=True)

    main, to_low, to_high, image_out = pl.pallas_call(
        grad_kernel,
        out_shape=(
            f32(channels, slabs, rows, cols),
            f32(channels, slabs, HALO, cols),
            f32(channels, slabs, HALO, cols),
            f32(views, channels, rows, cols),
        ),
        in_specs=[SMEM, SMEM, VMEM, VMEM, VMEM, VMEM],
        out_specs=(VMEM, VMEM, VMEM, VMEM),
        scratch_shapes=[
            pltpu.VMEM((views, slabs, channels, tiles, rows + 16, LANES), jnp.float32)
        ],
        name="grad",
    )(table, view_ids, got, absorb_part, emit_part, weights)
    from_low = lax.ppermute(to_high, "lat", up)
    from_high = lax.ppermute(to_low, "lat", down)
    grad_out = pl.pallas_call(
        join_kernel,
        out_shape=f32(channels, slabs, rows, cols),
        in_specs=[VMEM, VMEM, VMEM],
        out_specs=VMEM,
        name="join",
    )(main, from_low, from_high)
    return (image_out, grad_out)


def solution(mesh):
    in_specs = (P(None, "depth", "lat", None), P(None, "depth"), P(), P(None, None, "lat", None))
    out_specs = (P(None, None, "lat", None), P(None, "depth", "lat", None))
    return jax.shard_map(
        on_device, mesh=mesh, in_specs=in_specs, out_specs=out_specs, check_vma=False
    )
```

```python
import jax
import jax.numpy as jnp
from jax import lax
from jax.experimental import pallas as pl
from jax.experimental.pallas import tpu as pltpu
from jax.sharding import PartitionSpec as P

HALO = 4
LANES = 128
VMEM = pl.BlockSpec(memory_space=pltpu.VMEM)
SMEM = pl.BlockSpec(memory_space=pltpu.SMEM)


def slab_kernel(depth_total, offs, vids, vol, low, high, agg, ext):
    channels, slabs, rows, cols = vol.shape
    views = vids.shape[0]
    tiles = cols // LANES
    bands = rows // 8
    for c in range(channels):
        for k in range(slabs):
            for t in range(tiles):
                lanes = pl.ds(t * LANES, LANES)
                ext[c, k, t, 4:8, :] = low[c, k, :, lanes]
                ext[c, k, t, 8 : 8 + rows, :] = vol[c, k, :, lanes]
                ext[c, k, t, 8 + rows : 12 + rows, :] = high[c, k, :, lanes]
    for v in range(views):
        starts = [8 - offs[k, vids[v]] for k in range(slabs)]
        for t in range(tiles):
            transmit = jnp.ones((rows, LANES), jnp.float32)
            colour = [jnp.zeros((rows, LANES), jnp.float32) for _ in range(3)]
            for k in range(slabs):
                part = [ext[c, k, t, pl.ds(starts[k], rows), :] for c in range(channels)]
                keep = jnp.exp(part[3] * (-1.0 / depth_total))
                seen = transmit * (1.0 - keep)
                colour = [colour[c] + seen * part[c] for c in range(3)]
                transmit = transmit * keep
            for b in range(bands):
                owner = (v * bands + b) * tiles + t
                agg[owner, 0] = transmit[8 * b : 8 * b + 8]
                for c in range(3):
                    agg[owner, 1 + c] = colour[c][8 * b : 8 * b + 8]


def local_kernel(depth_total, offs, vids, ext, w, absorb_part, emit_part):
    channels, slabs, tiles = ext.shape[:3]
    views, _, rows, _ = w.shape
    for v in range(views):
        starts = [8 - offs[k, vids[v]] for k in range(slabs)]
        for t in range(tiles):
            lanes = pl.ds(t * LANES, LANES)
            weight = [w[v, c, :, lanes] for c in range(3)]
            transmit = jnp.ones((rows, LANES), jnp.float32)
            alphas, keeps, glows, fronts = [], [], [], []
            for k in range(slabs):
                part = [ext[c, k, t, pl.ds(starts[k], rows), :] for c in range(channels)]
                keep = jnp.exp(part[3] * (-1.0 / depth_total))
                alpha = 1.0 - keep
                emit_part[v, k, t] = transmit * alpha * float(depth_total)
                glows.append(weight[0] * part[0] + weight[1] * part[1] + weight[2] * part[2])
                alphas.append(alpha)
                keeps.append(keep)
                transmit = transmit * keep
                fronts.append(transmit)
            behind = jnp.zeros((rows, LANES), jnp.float32)
            for k in range(slabs - 1, -1, -1):
                absorb_part[v, k, t] = fronts[k] * (glows[k] - behind)
                behind = alphas[k] * glows[k] + keeps[k] * behind


def scan_kernel(place, agg, w, out):
    count = agg.shape[0]
    transmit = jnp.ones((8, LANES), jnp.float32)
    colour = [jnp.zeros((8, LANES), jnp.float32) for _ in range(3)]
    entering = []
    for s in range(count):
        entering.append(transmit)
        colour = [colour[c] + transmit * agg[s, 1 + c] for c in range(3)]
        transmit = transmit * agg[s, 0]
    picture = colour + [1.0 - transmit]
    behind = -w[0, 3]
    for s in range(count - 1, -1, -1):
        passed = agg[s, 0] * behind
        out[s, 0] = entering[s]
        out[s, 1] = entering[s] * passed
        for j in range(2):
            out[s, 2 + j] = picture[2 * (s % 2) + j]
        glow = w[0, 0] * agg[s, 1] + w[0, 1] * agg[s, 2] + w[0, 2] * agg[s, 3]
        behind = glow + passed


def pixel_grads(got, absorb_part, emit_part, w, v, t, tiles, bands, slabs):
    lanes = pl.ds(t * LANES, LANES)
    owners = [(v * bands + b) * tiles + t for b in range(bands)]
    front = jnp.concatenate([got[n, 0] for n in owners], axis=0)
    passed = jnp.concatenate([got[n, 1] for n in owners], axis=0)
    weight = [front * w[v, c, :, lanes] for c in range(3)]
    for k in range(slabs):
        emit = emit_part[v, k, t]
        parts = [emit * weight[c] for c in range(3)]
        parts.append(front * absorb_part[v, k, t] - passed)
        yield k, parts


def edge_kernel(offs, vids, got, absorb_part, emit_part, w, low, high, half, shifted):
    views, channels, rows, cols = w.shape
    slabs = low.shape[1]
    tiles = cols // LANES
    bands = rows // 8
    edge = jnp.zeros((8, LANES), jnp.float32)
    for n in range(got.shape[0]):
        half[n] = got[n, 2:4]
    moves = [[offs[k, vids[v]] for k in range(slabs)] for v in range(views)]
    for t in range(tiles):
        lanes = pl.ds(t * LANES, LANES)
        for v in range(views):
            grads = pixel_grads(got, absorb_part, emit_part, w, v, t, tiles, bands, slabs)
            for k, parts in grads:
                for c in range(channels):
                    shifted[v, k, c, t, 0:8, :] = edge
                    shifted[v, k, c, t, 8 : 8 + rows, :] = parts[c]
                    shifted[v, k, c, t, 8 + rows : 16 + rows, :] = edge
        for k in range(slabs):
            for c in range(channels):

                def total(start):
                    return sum(
                        shifted[v, k, c, t, pl.ds(start + moves[v][k], 4), :]
                        for v in range(views)
                    )

                low[c, k, :, lanes] = total(4)
                high[c, k, :, lanes] = total(8 + rows)


def main_kernel(offs, vids, got, absorb_part, emit_part, w, main, shifted):
    views, channels, rows, cols = w.shape
    slabs = main.shape[1]
    tiles = cols // LANES
    bands = rows // 8
    edge = jnp.zeros((4, LANES), jnp.float32)
    moves = [[offs[k, vids[v]] for k in range(slabs)] for v in range(views)]
    for t in range(tiles):
        lanes = pl.ds(t * LANES, LANES)
        for v in range(views):
            grads = pixel_grads(got, absorb_part, emit_part, w, v, t, tiles, bands, slabs)
            for k, parts in grads:
                for c in range(channels):
                    shifted[v, k, c, t, 4:8, :] = edge
                    shifted[v, k, c, t, 8 : 8 + rows, :] = parts[c]
                    shifted[v, k, c, t, 8 + rows : 12 + rows, :] = edge
        for k in range(slabs):
            for c in range(channels):
                main[c, k, :, lanes] = sum(
                    shifted[v, k, c, t, pl.ds(8 + moves[v][k], rows), :] for v in range(views)
                )


def join_kernel(place, main, low, high, mine, theirs, out, image):
    rows = main.shape[2]
    views, channels, _, cols = image.shape
    tiles = cols // LANES
    bands = rows // 8
    out[:, :, 0:4, :] = main[:, :, 0:4, :] + low[...]
    out[:, :, 4 : rows - 4, :] = main[:, :, 4 : rows - 4, :]
    out[:, :, rows - 4 :, :] = main[:, :, rows - 4 :, :] + high[...]
    first = 2 * (place[0] % 2)
    for v in range(views):
        for b in range(bands):
            for t in range(tiles):
                n = (v * bands + b) * tiles + t
                for j in range(2):
                    image[v, first + j, 8 * b : 8 * b + 8, t * LANES : (t + 1) * LANES] = mine[n, j]
                    image[v, 2 - first + j, 8 * b : 8 * b + 8, t * LANES : (t + 1) * LANES] = theirs[
                        n, j
                    ]


def on_chip(x):
    return pltpu.with_memory_space_constraint(x, pltpu.VMEM)


def on_device(volume, offsets, view_ids, weights):
    channels, slabs, rows, cols = volume.shape
    views = weights.shape[0]
    count = lax.axis_size("depth")
    strips = lax.axis_size("lat")
    tiles, bands = cols // LANES, rows // 8
    depth_total = slabs * count
    up = [(i, i + 1) for i in range(strips - 1)]
    down = [(i + 1, i) for i in range(strips - 1)]
    pair = [(i, i ^ 1) for i in range(count)]
    f32 = lambda *shape: jax.ShapeDtypeStruct(shape, jnp.float32)
    kept = lambda *shape: pltpu.VMEM(shape, jnp.float32)
    table = offsets.T
    place = lax.axis_index("depth").reshape(1).astype(jnp.int32)
    w = on_chip(weights)

    low = lax.ppermute(volume[:, :, rows - HALO :], "lat", up)
    high = lax.ppermute(volume[:, :, :HALO], "lat", down)
    agg, ext = pl.pallas_call(
        lambda *refs: slab_kernel(depth_total, *refs),
        out_shape=(kept(count, 4, 8, LANES), kept(channels, slabs, tiles, rows + 16, LANES)),
        in_specs=[SMEM, SMEM, VMEM, VMEM, VMEM],
        out_specs=(VMEM, VMEM),
        name="slab",
    )(table, view_ids, on_chip(volume), on_chip(low), on_chip(high))

    agg = lax.all_to_all(agg, "depth", 0, 0, tiled=True)
    absorb_part, emit_part = pl.pallas_call(
        lambda *refs: local_kernel(depth_total, *refs),
        out_shape=(
            kept(views, slabs, tiles, rows, LANES),
            kept(views, slabs, tiles, rows, LANES),
        ),
        in_specs=[SMEM, SMEM, VMEM, VMEM],
        out_specs=(VMEM, VMEM),
        name="local",
    )(table, view_ids, on_chip(ext), w)
    sent = pl.pallas_call(
        scan_kernel,
        out_shape=kept(count, 4, 8, LANES),
        grid_spec=pltpu.PrefetchScalarGridSpec(
            num_scalar_prefetch=1,
            grid=(1,),
            in_specs=[
                VMEM,
                pl.BlockSpec(
                    (1, 4, 8, LANES),
                    lambda i, z: (z[0] // (bands * tiles), 0, (z[0] // tiles) % bands, z[0] % tiles),
                ),
            ],
            out_specs=VMEM,
        ),
        name="scan",
    )(place, on_chip(agg), weights)
    got = on_chip(lax.all_to_all(sent, "depth", 0, 0, tiled=True))

    to_low, to_high, mine = pl.pallas_call(
        edge_kernel,
        out_shape=(
            kept(channels, slabs, HALO, cols),
            kept(channels, slabs, HALO, cols),
            kept(count, 2, 8, LANES),
        ),
        in_specs=[SMEM, SMEM, VMEM, VMEM, VMEM, VMEM],
        out_specs=(VMEM, VMEM, VMEM),
        scratch_shapes=[
            pltpu.VMEM((views, slabs, channels, tiles, rows + 16, LANES), jnp.float32)
        ],
        name="edge",
    )(table, view_ids, got, on_chip(absorb_part), on_chip(emit_part), w)
    from_low = lax.ppermute(to_high, "lat", up)
    from_high = lax.ppermute(to_low, "lat", down)
    theirs = lax.ppermute(mine, "depth", pair)
    main = pl.pallas_call(
        main_kernel,
        out_shape=kept(channels, slabs, rows, cols),
        in_specs=[SMEM, SMEM, VMEM, VMEM, VMEM, VMEM],
        out_specs=VMEM,
        scratch_shapes=[
            pltpu.VMEM((views, slabs, channels, tiles, rows + 16, LANES), jnp.float32)
        ],
        name="main",
    )(table, view_ids, got, on_chip(absorb_part), on_chip(emit_part), w)
    grad_out, image_out = pl.pallas_call(
        join_kernel,
        out_shape=(f32(channels, slabs, rows, cols), f32(views, channels, rows, cols)),
        in_specs=[SMEM, VMEM, VMEM, VMEM, VMEM, VMEM],
        out_specs=(VMEM, VMEM),
        name="join",
    )(place, on_chip(main), on_chip(from_low), on_chip(from_high), on_chip(mine), on_chip(theirs))
    return (image_out, grad_out)


def solution(mesh):
    in_specs = (P(None, "depth", "lat", None), P(None, "depth"), P(), P(None, None, "lat", None))
    out_specs = (P(None, None, "lat", None), P(None, "depth", "lat", None))
    return jax.shard_map(
        on_device, mesh=mesh, in_specs=in_specs, out_specs=out_specs, check_vma=False
    )
```

```python
import jax
import jax.numpy as jnp
from jax import lax
from jax.experimental import pallas as pl
from jax.experimental.pallas import tpu as pltpu
from jax.sharding import PartitionSpec as P

HALO = 4
LANES = 128
VMEM = pl.BlockSpec(memory_space=pltpu.VMEM)
SMEM = pl.BlockSpec(memory_space=pltpu.SMEM)


def slab_kernel(depth_total, offs, vids, vol, low, high, agg, ext):
    channels, slabs, rows, cols = vol.shape
    views = vids.shape[0]
    tiles = cols // LANES
    bands = rows // 8
    for c in range(channels):
        for k in range(slabs):
            for t in range(tiles):
                lanes = pl.ds(t * LANES, LANES)
                ext[c, k, t, 4:8, :] = low[c, k, :, lanes]
                ext[c, k, t, 8 : 8 + rows, :] = vol[c, k, :, lanes]
                ext[c, k, t, 8 + rows : 12 + rows, :] = high[c, k, :, lanes]
    for v in range(views):
        starts = [8 - offs[k, vids[v]] for k in range(slabs)]
        for t in range(tiles):
            transmit = jnp.ones((rows, LANES), jnp.float32)
            colour = [jnp.zeros((rows, LANES), jnp.float32) for _ in range(3)]
            for k in range(slabs):
                part = [ext[c, k, t, pl.ds(starts[k], rows), :] for c in range(channels)]
                keep = jnp.exp(part[3] * (-1.0 / depth_total))
                seen = transmit * (1.0 - keep)
                colour = [colour[c] + seen * part[c] for c in range(3)]
                transmit = transmit * keep
            for b in range(bands):
                owner = v * bands + b
                agg[owner, 0, t] = transmit[8 * b : 8 * b + 8]
                for c in range(3):
                    agg[owner, 1 + c, t] = colour[c][8 * b : 8 * b + 8]


def local_kernel(depth_total, offs, vids, ext, w, absorb_part, emit_part):
    channels, slabs, tiles = ext.shape[:3]
    views, _, rows, _ = w.shape
    for v in range(views):
        starts = [8 - offs[k, vids[v]] for k in range(slabs)]
        for t in range(tiles):
            lanes = pl.ds(t * LANES, LANES)
            weight = [w[v, c, :, lanes] for c in range(3)]
            transmit = jnp.ones((rows, LANES), jnp.float32)
            alphas, keeps, glows, fronts = [], [], [], []
            for k in range(slabs):
                part = [ext[c, k, t, pl.ds(starts[k], rows), :] for c in range(channels)]
                keep = jnp.exp(part[3] * (-1.0 / depth_total))
                alpha = 1.0 - keep
                emit_part[v, k, t] = transmit * alpha * float(depth_total)
                glows.append(weight[0] * part[0] + weight[1] * part[1] + weight[2] * part[2])
                alphas.append(alpha)
                keeps.append(keep)
                transmit = transmit * keep
                fronts.append(transmit)
            behind = jnp.zeros((rows, LANES), jnp.float32)
            for k in range(slabs - 1, -1, -1):
                absorb_part[v, k, t] = fronts[k] * (glows[k] - behind)
                behind = alphas[k] * glows[k] + keeps[k] * behind


def seat(place, members):
    mine, member = lax.div(place[0], members), lax.rem(place[0], members)
    turned = (mine == 1) | (mine == 2)
    order = [jnp.where(turned, members - 1 - j, j) for j in range(members)]
    return mine, jnp.where(turned, members - 1 - member, member), order


def group_kernel(place, agg, out):
    members, _, tiles = agg.shape[:3]
    _, _, order = seat(place, members)
    for t in range(tiles):
        transmit = agg[order[0], 0, t]
        colour = [agg[order[0], 1 + c, t] for c in range(3)]
        for j in range(1, members):
            colour = [colour[c] + transmit * agg[order[j], 1 + c, t] for c in range(3)]
            transmit = transmit * agg[order[j], 0, t]
        for n in range(out.shape[0]):
            out[n, 0, t] = transmit
            for c in range(3):
                out[n, 1 + c, t] = colour[c]


def scan_kernel(place, agg, groups, w, out):
    members, _, tiles = agg.shape[:3]
    mine, owner, order = seat(place, members)
    bands = w.shape[2] // 8
    view, band = lax.div(owner, bands), lax.rem(owner, bands)
    rows = pl.ds(pl.multiple_of(8 * band, 8), 8)
    for t in range(tiles):
        lanes = pl.ds(t * LANES, LANES)
        weight = [w[view, c, rows, lanes] for c in range(4)]
        transmit = jnp.ones((8, LANES), jnp.float32)
        colour = [jnp.zeros((8, LANES), jnp.float32) for _ in range(3)]
        front = transmit
        count = groups.shape[0]
        for g in range(count):
            front = jnp.where(mine == g, transmit, front)
            colour = [colour[c] + transmit * groups[g, 1 + c, t] for c in range(3)]
            transmit = transmit * groups[g, 0, t]
        picture = colour + [1.0 - transmit]
        behind = -weight[3]
        enter = behind
        for g in range(count - 1, 0, -1):
            glow = sum(weight[c] * groups[g, 1 + c, t] for c in range(3))
            behind = glow + groups[g, 0, t] * behind
            enter = jnp.where(mine == g - 1, behind, enter)
        fronts = []
        for j in range(members):
            fronts.append(front)
            front = front * agg[order[j], 0, t]
        for j in range(members - 1, -1, -1):
            passed = agg[order[j], 0, t] * enter
            out[order[j], 0, t] = fronts[j]
            out[order[j], 1, t] = fronts[j] * passed
            for c in range(4):
                out[order[j], 2 + c, t] = picture[c]
            enter = passed + sum(weight[c] * agg[order[j], 1 + c, t] for c in range(3))


def pixel_grads(got, absorb_part, emit_part, w, v, t, tiles, bands, slabs):
    lanes = pl.ds(t * LANES, LANES)
    owners = [v * bands + b for b in range(bands)]
    front = jnp.concatenate([got[n, 0, t] for n in owners], axis=0)
    passed = jnp.concatenate([got[n, 1, t] for n in owners], axis=0)
    weight = [front * w[v, c, :, lanes] for c in range(3)]
    for k in range(slabs):
        emit = emit_part[v, k, t]
        parts = [emit * weight[c] for c in range(3)]
        parts.append(front * absorb_part[v, k, t] - passed)
        yield k, parts


def edge_kernel(offs, vids, got, absorb_part, emit_part, w, low, high, shifted):
    views, channels, rows, cols = w.shape
    slabs = low.shape[1]
    tiles = cols // LANES
    bands = rows // 8
    edge = jnp.zeros((8, LANES), jnp.float32)
    moves = [[offs[k, vids[v]] for k in range(slabs)] for v in range(views)]
    for t in range(tiles):
        lanes = pl.ds(t * LANES, LANES)
        for v in range(views):
            grads = pixel_grads(got, absorb_part, emit_part, w, v, t, tiles, bands, slabs)
            for k, parts in grads:
                for c in range(channels):
                    shifted[v, k, c, t, 0:8, :] = edge
                    shifted[v, k, c, t, 8 : 8 + rows, :] = parts[c]
                    shifted[v, k, c, t, 8 + rows : 16 + rows, :] = edge
        for k in range(slabs):
            for c in range(channels):

                def total(start):
                    return sum(
                        shifted[v, k, c, t, pl.ds(start + moves[v][k], 4), :]
                        for v in range(views)
                    )

                low[c, k, :, lanes] = total(4)
                high[c, k, :, lanes] = total(8 + rows)


def main_kernel(offs, vids, got, absorb_part, emit_part, w, main, shifted):
    views, channels, rows, cols = w.shape
    slabs = main.shape[1]
    tiles = cols // LANES
    bands = rows // 8
    edge = jnp.zeros((4, LANES), jnp.float32)
    moves = [[offs[k, vids[v]] for k in range(slabs)] for v in range(views)]
    for t in range(tiles):
        lanes = pl.ds(t * LANES, LANES)
        for v in range(views):
            grads = pixel_grads(got, absorb_part, emit_part, w, v, t, tiles, bands, slabs)
            for k, parts in grads:
                for c in range(channels):
                    shifted[v, k, c, t, 4:8, :] = edge
                    shifted[v, k, c, t, 8 : 8 + rows, :] = parts[c]
                    shifted[v, k, c, t, 8 + rows : 12 + rows, :] = edge
        for k in range(slabs):
            for c in range(channels):
                main[c, k, :, lanes] = sum(
                    shifted[v, k, c, t, pl.ds(8 + moves[v][k], rows), :] for v in range(views)
                )


def join_kernel(main, low, high, got, out, image):
    rows = main.shape[2]
    views, channels, _, cols = image.shape
    bands = rows // 8
    out[:, :, 0:4, :] = main[:, :, 0:4, :] + low[...]
    out[:, :, 4 : rows - 4, :] = main[:, :, 4 : rows - 4, :]
    out[:, :, rows - 4 :, :] = main[:, :, rows - 4 :, :] + high[...]
    for v in range(views):
        for b in range(bands):
            for t in range(cols // LANES):
                for c in range(channels):
                    image[v, c, 8 * b : 8 * b + 8, t * LANES : (t + 1) * LANES] = got[
                        v * bands + b, 2 + c, t
                    ]


def on_chip(x):
    return pltpu.with_memory_space_constraint(x, pltpu.VMEM)


def on_device(volume, offsets, view_ids, weights):
    channels, slabs, rows, cols = volume.shape
    views = weights.shape[0]
    count = lax.axis_size("depth")
    strips = lax.axis_size("lat")
    tiles, bands = cols // LANES, rows // 8
    depth_total = slabs * count
    size = views * bands
    near = [[size * g + i for i in range(size)] for g in range(count // size)]
    near = [row[::-1] if g in (1, 2) else row for g, row in enumerate(near)]
    far = [[row[i] for row in near] for i in range(size)]
    up = [(i, i + 1) for i in range(strips - 1)]
    down = [(i + 1, i) for i in range(strips - 1)]
    f32 = lambda *shape: jax.ShapeDtypeStruct(shape, jnp.float32)
    kept = lambda *shape: pltpu.VMEM(shape, jnp.float32)
    table = offsets.T
    place = lax.axis_index("depth").reshape(1).astype(jnp.int32)
    w = on_chip(weights)

    def swap(x, groups):
        return lax.all_to_all(x, "depth", 0, 0, tiled=True, axis_index_groups=groups)

    low = lax.ppermute(volume[:, :, rows - HALO :], "lat", up)
    high = lax.ppermute(volume[:, :, :HALO], "lat", down)
    agg, ext = pl.pallas_call(
        lambda *refs: slab_kernel(depth_total, *refs),
        out_shape=(
            kept(size, 4, tiles, 8, LANES),
            kept(channels, slabs, tiles, rows + 16, LANES),
        ),
        in_specs=[SMEM, SMEM, VMEM, VMEM, VMEM],
        out_specs=(VMEM, VMEM),
        name="slab",
    )(table, view_ids, on_chip(volume), on_chip(low), on_chip(high))
    agg = on_chip(swap(agg, near))
    grouped = pl.pallas_call(
        group_kernel,
        out_shape=kept(count // size, 4, tiles, 8, LANES),
        in_specs=[SMEM, VMEM],
        out_specs=VMEM,
        name="group",
    )(place, agg)
    groups = on_chip(swap(grouped, far))
    absorb_part, emit_part = pl.pallas_call(
        lambda *refs: local_kernel(depth_total, *refs),
        out_shape=(
            kept(views, slabs, tiles, rows, LANES),
            kept(views, slabs, tiles, rows, LANES),
        ),
        in_specs=[SMEM, SMEM, VMEM, VMEM],
        out_specs=(VMEM, VMEM),
        name="local",
    )(table, view_ids, on_chip(ext), w)
    sent = pl.pallas_call(
        scan_kernel,
        out_shape=kept(size, 6, tiles, 8, LANES),
        in_specs=[SMEM, VMEM, VMEM, VMEM],
        out_specs=VMEM,
        name="scan",
    )(place, agg, groups, w)
    got = on_chip(swap(sent, near))

    to_low, to_high = pl.pallas_call(
        edge_kernel,
        out_shape=(
            kept(channels, slabs, HALO, cols),
            kept(channels, slabs, HALO, cols),
        ),
        in_specs=[SMEM, SMEM, VMEM, VMEM, VMEM, VMEM],
        out_specs=(VMEM, VMEM),
        scratch_shapes=[
            pltpu.VMEM((views, slabs, channels, tiles, rows + 16, LANES), jnp.float32)
        ],
        name="edge",
    )(table, view_ids, got, on_chip(absorb_part), on_chip(emit_part), w)
    from_low = lax.ppermute(to_high, "lat", up)
    from_high = lax.ppermute(to_low, "lat", down)
    main = pl.pallas_call(
        main_kernel,
        out_shape=kept(channels, slabs, rows, cols),
        in_specs=[SMEM, SMEM, VMEM, VMEM, VMEM, VMEM],
        out_specs=VMEM,
        scratch_shapes=[
            pltpu.VMEM((views, slabs, channels, tiles, rows + 16, LANES), jnp.float32)
        ],
        name="main",
    )(table, view_ids, got, on_chip(absorb_part), on_chip(emit_part), w)
    grad_out, image_out = pl.pallas_call(
        join_kernel,
        out_shape=(f32(channels, slabs, rows, cols), f32(views, channels, rows, cols)),
        in_specs=[VMEM, VMEM, VMEM, VMEM],
        out_specs=(VMEM, VMEM),
        name="join",
    )(on_chip(main), on_chip(from_low), on_chip(from_high), got)
    return (image_out, grad_out)


def solution(mesh):
    in_specs = (P(None, "depth", "lat", None), P(None, "depth"), P(), P(None, None, "lat", None))
    out_specs = (P(None, None, "lat", None), P(None, "depth", "lat", None))
    return jax.shard_map(
        on_device, mesh=mesh, in_specs=in_specs, out_specs=out_specs, check_vma=False
    )
```

```python
import jax
import jax.numpy as jnp
from jax import lax
from jax.experimental import pallas as pl
from jax.experimental.pallas import tpu as pltpu
from jax.sharding import PartitionSpec as P

HALO = 4
LANES = 128
VMEM = pl.BlockSpec(memory_space=pltpu.VMEM)
SMEM = pl.BlockSpec(memory_space=pltpu.SMEM)


def slab_kernel(depth_total, offs, vids, vol, low, high, agg, ext):
    channels, slabs, rows, cols = vol.shape
    views = vids.shape[0]
    tiles = cols // LANES
    bands = rows // 8
    for c in range(channels):
        for k in range(slabs):
            for t in range(tiles):
                lanes = pl.ds(t * LANES, LANES)
                ext[c, k, t, 4:8, :] = low[c, k, :, lanes]
                ext[c, k, t, 8 : 8 + rows, :] = vol[c, k, :, lanes]
                ext[c, k, t, 8 + rows : 12 + rows, :] = high[c, k, :, lanes]
    for v in range(views):
        starts = [8 - offs[k, vids[v]] for k in range(slabs)]
        for t in range(tiles):
            transmit = jnp.ones((rows, LANES), jnp.float32)
            colour = [jnp.zeros((rows, LANES), jnp.float32) for _ in range(3)]
            for k in range(slabs):
                part = [ext[c, k, t, pl.ds(starts[k], rows), :] for c in range(channels)]
                keep = jnp.exp(part[3] * (-1.0 / depth_total))
                seen = transmit * (1.0 - keep)
                colour = [colour[c] + seen * part[c] for c in range(3)]
                transmit = transmit * keep
            for b in range(bands):
                owner = v * bands + b
                agg[owner, 0, t] = transmit[8 * b : 8 * b + 8]
                for c in range(3):
                    agg[owner, 1 + c, t] = colour[c][8 * b : 8 * b + 8]


def local_kernel(depth_total, offs, vids, ext, w, absorb_part, emit_part):
    channels, slabs, tiles = ext.shape[:3]
    views, _, rows, _ = w.shape
    for v in range(views):
        starts = [8 - offs[k, vids[v]] for k in range(slabs)]
        for t in range(tiles):
            lanes = pl.ds(t * LANES, LANES)
            weight = [w[v, c, :, lanes] for c in range(3)]
            transmit = jnp.ones((rows, LANES), jnp.float32)
            alphas, keeps, glows, fronts = [], [], [], []
            for k in range(slabs):
                part = [ext[c, k, t, pl.ds(starts[k], rows), :] for c in range(channels)]
                keep = jnp.exp(part[3] * (-1.0 / depth_total))
                alpha = 1.0 - keep
                emit_part[v, k, t] = transmit * alpha * float(depth_total)
                glows.append(weight[0] * part[0] + weight[1] * part[1] + weight[2] * part[2])
                alphas.append(alpha)
                keeps.append(keep)
                transmit = transmit * keep
                fronts.append(transmit)
            behind = jnp.zeros((rows, LANES), jnp.float32)
            for k in range(slabs - 1, -1, -1):
                absorb_part[v, k, t] = fronts[k] * (glows[k] - behind)
                behind = alphas[k] * glows[k] + keeps[k] * behind


def seat(place, members):
    mine, member = lax.div(place[0], members), lax.rem(place[0], members)
    turned = (mine == 1) | (mine == 2)
    order = [jnp.where(turned, members - 1 - j, j) for j in range(members)]
    return mine, jnp.where(turned, members - 1 - member, member), order


def group_kernel(place, agg, out):
    members, _, tiles = agg.shape[:3]
    _, _, order = seat(place, members)
    for t in range(tiles):
        transmit = agg[order[0], 0, t]
        colour = [agg[order[0], 1 + c, t] for c in range(3)]
        for j in range(1, members):
            colour = [colour[c] + transmit * agg[order[j], 1 + c, t] for c in range(3)]
            transmit = transmit * agg[order[j], 0, t]
        for n in range(out.shape[0]):
            out[n, 0, t] = transmit
            for c in range(3):
                out[n, 1 + c, t] = colour[c]


def scan_kernel(place, agg, groups, w, out, shown):
    members, _, tiles = agg.shape[:3]
    mine, owner, order = seat(place, members)
    bands = w.shape[2] // 8
    view, band = lax.div(owner, bands), lax.rem(owner, bands)
    rows = pl.ds(pl.multiple_of(8 * band, 8), 8)
    for t in range(tiles):
        lanes = pl.ds(t * LANES, LANES)
        weight = [w[view, c, rows, lanes] for c in range(4)]
        transmit = jnp.ones((8, LANES), jnp.float32)
        colour = [jnp.zeros((8, LANES), jnp.float32) for _ in range(3)]
        front = transmit
        count = groups.shape[0]
        for g in range(count):
            front = jnp.where(mine == g, transmit, front)
            colour = [colour[c] + transmit * groups[g, 1 + c, t] for c in range(3)]
            transmit = transmit * groups[g, 0, t]
        picture = colour + [1.0 - transmit]
        behind = -weight[3]
        enter = behind
        for g in range(count - 1, 0, -1):
            glow = sum(weight[c] * groups[g, 1 + c, t] for c in range(3))
            behind = glow + groups[g, 0, t] * behind
            enter = jnp.where(mine == g - 1, behind, enter)
        fronts = []
        for j in range(members):
            fronts.append(front)
            front = front * agg[order[j], 0, t]
        for j in range(members - 1, -1, -1):
            passed = agg[order[j], 0, t] * enter
            out[order[j], 0, t] = fronts[j]
            out[order[j], 1, t] = fronts[j] * passed
            for c in range(4):
                shown[j, c, t] = picture[c]
            enter = passed + sum(weight[c] * agg[order[j], 1 + c, t] for c in range(3))


def pixel_grads(got, absorb_part, emit_part, w, v, t, tiles, bands, slabs):
    lanes = pl.ds(t * LANES, LANES)
    owners = [v * bands + b for b in range(bands)]
    front = jnp.concatenate([got[n, 0, t] for n in owners], axis=0)
    passed = jnp.concatenate([got[n, 1, t] for n in owners], axis=0)
    weight = [front * w[v, c, :, lanes] for c in range(3)]
    for k in range(slabs):
        emit = emit_part[v, k, t]
        parts = [emit * weight[c] for c in range(3)]
        parts.append(front * absorb_part[v, k, t] - passed)
        yield k, parts


def edge_kernel(offs, vids, got, absorb_part, emit_part, w, low, high, shifted):
    views, channels, rows, cols = w.shape
    slabs = low.shape[1]
    tiles = cols // LANES
    bands = rows // 8
    edge = jnp.zeros((8, LANES), jnp.float32)
    moves = [[offs[k, vids[v]] for k in range(slabs)] for v in range(views)]
    for t in range(tiles):
        lanes = pl.ds(t * LANES, LANES)
        for v in range(views):
            grads = pixel_grads(got, absorb_part, emit_part, w, v, t, tiles, bands, slabs)
            for k, parts in grads:
                for c in range(channels):
                    shifted[v, k, c, t, 0:8, :] = edge
                    shifted[v, k, c, t, 8 : 8 + rows, :] = parts[c]
                    shifted[v, k, c, t, 8 + rows : 16 + rows, :] = edge
        for k in range(slabs):
            for c in range(channels):

                def total(start):
                    return sum(
                        shifted[v, k, c, t, pl.ds(start + moves[v][k], 4), :]
                        for v in range(views)
                    )

                low[c, k, :, lanes] = total(4)
                high[c, k, :, lanes] = total(8 + rows)


def main_kernel(offs, vids, got, absorb_part, emit_part, w, main, shifted):
    views, channels, rows, cols = w.shape
    slabs = main.shape[1]
    tiles = cols // LANES
    bands = rows // 8
    edge = jnp.zeros((4, LANES), jnp.float32)
    moves = [[offs[k, vids[v]] for k in range(slabs)] for v in range(views)]
    for t in range(tiles):
        lanes = pl.ds(t * LANES, LANES)
        for v in range(views):
            grads = pixel_grads(got, absorb_part, emit_part, w, v, t, tiles, bands, slabs)
            for k, parts in grads:
                for c in range(channels):
                    shifted[v, k, c, t, 4:8, :] = edge
                    shifted[v, k, c, t, 8 : 8 + rows, :] = parts[c]
                    shifted[v, k, c, t, 8 + rows : 12 + rows, :] = edge
        for k in range(slabs):
            for c in range(channels):
                main[c, k, :, lanes] = sum(
                    shifted[v, k, c, t, pl.ds(8 + moves[v][k], rows), :] for v in range(views)
                )


def join_kernel(main, low, high, shown, out, image):
    rows = main.shape[2]
    views, channels, _, cols = image.shape
    bands = rows // 8
    out[:, :, 0:4, :] = main[:, :, 0:4, :] + low[...]
    out[:, :, 4 : rows - 4, :] = main[:, :, 4 : rows - 4, :]
    out[:, :, rows - 4 :, :] = main[:, :, rows - 4 :, :] + high[...]
    for v in range(views):
        for b in range(bands):
            for t in range(cols // LANES):
                for c in range(channels):
                    image[v, c, 8 * b : 8 * b + 8, t * LANES : (t + 1) * LANES] = shown[
                        v * bands + b, c, t
                    ]


def on_chip(x):
    return pltpu.with_memory_space_constraint(x, pltpu.VMEM)


def on_device(volume, offsets, view_ids, weights):
    channels, slabs, rows, cols = volume.shape
    views = weights.shape[0]
    count = lax.axis_size("depth")
    strips = lax.axis_size("lat")
    tiles, bands = cols // LANES, rows // 8
    depth_total = slabs * count
    size = views * bands
    near = [[size * g + i for i in range(size)] for g in range(count // size)]
    near = [row[::-1] if g in (1, 2) else row for g, row in enumerate(near)]
    far = [[row[i] for row in near] for i in range(size)]
    up = [(i, i + 1) for i in range(strips - 1)]
    down = [(i + 1, i) for i in range(strips - 1)]
    f32 = lambda *shape: jax.ShapeDtypeStruct(shape, jnp.float32)
    kept = lambda *shape: pltpu.VMEM(shape, jnp.float32)
    table = offsets.T
    place = lax.axis_index("depth").reshape(1).astype(jnp.int32)
    w = on_chip(weights)

    def swap(x, groups):
        return lax.all_to_all(x, "depth", 0, 0, tiled=True, axis_index_groups=groups)

    low = lax.ppermute(volume[:, :, rows - HALO :], "lat", up)
    high = lax.ppermute(volume[:, :, :HALO], "lat", down)
    agg, ext = pl.pallas_call(
        lambda *refs: slab_kernel(depth_total, *refs),
        out_shape=(
            kept(size, 4, tiles, 8, LANES),
            kept(channels, slabs, tiles, rows + 16, LANES),
        ),
        in_specs=[SMEM, SMEM, VMEM, VMEM, VMEM],
        out_specs=(VMEM, VMEM),
        name="slab",
    )(table, view_ids, on_chip(volume), on_chip(low), on_chip(high))
    agg = on_chip(swap(agg, near))
    grouped = pl.pallas_call(
        group_kernel,
        out_shape=kept(count // size, 4, tiles, 8, LANES),
        in_specs=[SMEM, VMEM],
        out_specs=VMEM,
        name="group",
    )(place, agg)
    groups = on_chip(swap(grouped, far))
    absorb_part, emit_part = pl.pallas_call(
        lambda *refs: local_kernel(depth_total, *refs),
        out_shape=(
            kept(views, slabs, tiles, rows, LANES),
            kept(views, slabs, tiles, rows, LANES),
        ),
        in_specs=[SMEM, SMEM, VMEM, VMEM],
        out_specs=(VMEM, VMEM),
        name="local",
    )(table, view_ids, on_chip(ext), w)
    sent, shown = pl.pallas_call(
        scan_kernel,
        out_shape=(kept(size, 2, tiles, 8, LANES), kept(size, 4, tiles, 8, LANES)),
        in_specs=[SMEM, VMEM, VMEM, VMEM],
        out_specs=(VMEM, VMEM),
        name="scan",
    )(place, agg, groups, w)
    got = on_chip(swap(sent, near))
    shown = swap(shown, near)

    to_low, to_high = pl.pallas_call(
        edge_kernel,
        out_shape=(
            kept(channels, slabs, HALO, cols),
            kept(channels, slabs, HALO, cols),
        ),
        in_specs=[SMEM, SMEM, VMEM, VMEM, VMEM, VMEM],
        out_specs=(VMEM, VMEM),
        scratch_shapes=[
            pltpu.VMEM((views, slabs, channels, tiles, rows + 16, LANES), jnp.float32)
        ],
        name="edge",
    )(table, view_ids, got, on_chip(absorb_part), on_chip(emit_part), w)
    from_low = lax.ppermute(to_high, "lat", up)
    from_high = lax.ppermute(to_low, "lat", down)
    main = pl.pallas_call(
        main_kernel,
        out_shape=kept(channels, slabs, rows, cols),
        in_specs=[SMEM, SMEM, VMEM, VMEM, VMEM, VMEM],
        out_specs=VMEM,
        scratch_shapes=[
            pltpu.VMEM((views, slabs, channels, tiles, rows + 16, LANES), jnp.float32)
        ],
        name="main",
    )(table, view_ids, got, on_chip(absorb_part), on_chip(emit_part), w)
    grad_out, image_out = pl.pallas_call(
        join_kernel,
        out_shape=(f32(channels, slabs, rows, cols), f32(views, channels, rows, cols)),
        in_specs=[VMEM, VMEM, VMEM, VMEM],
        out_specs=(VMEM, VMEM),
        name="join",
    )(on_chip(main), on_chip(from_low), on_chip(from_high), on_chip(shown))
    return (image_out, grad_out)


def solution(mesh):
    in_specs = (P(None, "depth", "lat", None), P(None, "depth"), P(), P(None, None, "lat", None))
    out_specs = (P(None, None, "lat", None), P(None, "depth", "lat", None))
    return jax.shard_map(
        on_device, mesh=mesh, in_specs=in_specs, out_specs=out_specs, check_vma=False
    )
```

```python
import jax
import jax.numpy as jnp
from jax import lax
from jax.experimental import pallas as pl
from jax.experimental.pallas import tpu as pltpu
from jax.sharding import PartitionSpec as P


HALO = 4
LANES = 128
VMEM = pl.BlockSpec(memory_space=pltpu.VMEM)
SMEM = pl.BlockSpec(memory_space=pltpu.SMEM)
LIMIT = pltpu.CompilerParams(vmem_limit_bytes=16 * 1024 * 1024)


def fill_kernel(vol, ext):
    channels, slabs, rows, cols = vol.shape
    for c in range(channels):
        for k in range(slabs):
            for t in range(cols // LANES):
                ext[c, k, t, 8 : 8 + rows, :] = vol[c, k, :, pl.ds(t * LANES, LANES)]


def slab_kernel(depth_total, offs, vids, strip, inner, outer, own, agg, ext):
    del own
    channels, slabs, tiles, rows = ext.shape[:4]
    rows -= 16
    views = vids.shape[0]
    bands = rows // 8
    odd = lax.rem(strip[0], 2) == 1
    for c in range(channels):
        for k in range(slabs):
            for t in range(tiles):
                lanes = pl.ds(t * LANES, LANES)
                near, far = inner[c, k, :, lanes], outer[c, k, :, lanes]
                ext[c, k, t, 4:8, :] = jnp.where(odd, near, far)
                ext[c, k, t, 8 + rows : 12 + rows, :] = jnp.where(odd, far, near)
    for v in range(views):
        starts = [8 - offs[k, vids[v]] for k in range(slabs)]
        for t in range(tiles):
            transmit = jnp.ones((rows, LANES), jnp.float32)
            colour = [jnp.zeros((rows, LANES), jnp.float32) for _ in range(3)]
            for k in range(slabs):
                part = [ext[c, k, t, pl.ds(starts[k], rows), :] for c in range(channels)]
                keep = jnp.exp(part[3] * (-1.0 / depth_total))
                seen = transmit * (1.0 - keep)
                colour = [colour[c] + seen * part[c] for c in range(3)]
                transmit = transmit * keep
            for b in range(bands):
                owner = v * bands + b
                agg[owner, 0, t] = transmit[8 * b : 8 * b + 8]
                for c in range(3):
                    agg[owner, 1 + c, t] = colour[c][8 * b : 8 * b + 8]


def local_kernel(depth_total, offs, vids, ext, w, absorb_part, emit_part):
    channels, slabs, tiles = ext.shape[:3]
    views, _, rows, _ = w.shape
    for v in range(views):
        starts = [8 - offs[k, vids[v]] for k in range(slabs)]
        for t in range(tiles):
            lanes = pl.ds(t * LANES, LANES)
            weight = [w[v, c, :, lanes] for c in range(3)]
            transmit = jnp.ones((rows, LANES), jnp.float32)
            alphas, keeps, glows, fronts = [], [], [], []
            for k in range(slabs):
                part = [ext[c, k, t, pl.ds(starts[k], rows), :] for c in range(channels)]
                keep = jnp.exp(part[3] * (-1.0 / depth_total))
                alpha = 1.0 - keep
                emit_part[v, k, t] = transmit * alpha * float(depth_total)
                glows.append(weight[0] * part[0] + weight[1] * part[1] + weight[2] * part[2])
                alphas.append(alpha)
                keeps.append(keep)
                transmit = transmit * keep
                fronts.append(transmit)
            behind = jnp.zeros((rows, LANES), jnp.float32)
            for k in range(slabs - 1, -1, -1):
                absorb_part[v, k, t] = fronts[k] * (glows[k] - behind)
                behind = alphas[k] * glows[k] + keeps[k] * behind


def seat(place, members):
    mine, member = lax.div(place[0], members), lax.rem(place[0], members)
    turned = (mine == 1) | (mine == 2)
    order = [jnp.where(turned, members - 1 - j, j) for j in range(members)]
    return mine, jnp.where(turned, members - 1 - member, member), order


def group_kernel(place, agg, out):
    members, _, tiles = agg.shape[:3]
    _, _, order = seat(place, members)
    for t in range(tiles):
        transmit = agg[order[0], 0, t]
        colour = [agg[order[0], 1 + c, t] for c in range(3)]
        for j in range(1, members):
            colour = [colour[c] + transmit * agg[order[j], 1 + c, t] for c in range(3)]
            transmit = transmit * agg[order[j], 0, t]
        for n in range(out.shape[0]):
            out[n, 0, t] = transmit
            for c in range(3):
                out[n, 1 + c, t] = colour[c]


def scan_kernel(place, agg, groups, w, out, shown):
    members, _, tiles = agg.shape[:3]
    mine, owner, order = seat(place, members)
    bands = w.shape[2] // 8
    view, band = lax.div(owner, bands), lax.rem(owner, bands)
    rows = pl.ds(pl.multiple_of(8 * band, 8), 8)
    for t in range(tiles):
        lanes = pl.ds(t * LANES, LANES)
        weight = [w[view, c, rows, lanes] for c in range(4)]
        transmit = jnp.ones((8, LANES), jnp.float32)
        colour = [jnp.zeros((8, LANES), jnp.float32) for _ in range(3)]
        front = transmit
        count = groups.shape[0]
        for g in range(count):
            front = jnp.where(mine == g, transmit, front)
            colour = [colour[c] + transmit * groups[g, 1 + c, t] for c in range(3)]
            transmit = transmit * groups[g, 0, t]
        picture = colour + [1.0 - transmit]
        behind = -weight[3]
        enter = behind
        for g in range(count - 1, 0, -1):
            glow = sum(weight[c] * groups[g, 1 + c, t] for c in range(3))
            behind = glow + groups[g, 0, t] * behind
            enter = jnp.where(mine == g - 1, behind, enter)
        fronts = []
        for j in range(members):
            fronts.append(front)
            front = front * agg[order[j], 0, t]
        for j in range(members - 1, -1, -1):
            passed = agg[order[j], 0, t] * enter
            out[order[j], 0, t] = fronts[j]
            out[order[j], 1, t] = fronts[j] * passed
            for c in range(4):
                shown[j, c, t] = picture[c]
            enter = passed + sum(weight[c] * agg[order[j], 1 + c, t] for c in range(3))


def pixel_grads(got, absorb_part, emit_part, w, v, t, bands, slabs):
    lanes = pl.ds(t * LANES, LANES)
    owners = [v * bands + b for b in range(bands)]
    front = jnp.concatenate([got[n, 0, t] for n in owners], axis=0)
    passed = jnp.concatenate([got[n, 1, t] for n in owners], axis=0)
    weight = [front * w[v, c, :, lanes] for c in range(3)]
    for k in range(slabs):
        emit = emit_part[v, k, t]
        parts = [emit * weight[c] for c in range(3)]
        parts.append(front * absorb_part[v, k, t] - passed)
        yield k, parts


def edge_kernel(offs, vids, strip, got, absorb_part, emit_part, w, inner, outer, shifted):
    views, channels, rows, cols = w.shape
    slabs = inner.shape[1]
    tiles = cols // LANES
    bands = rows // 8
    odd = lax.rem(strip[0], 2) == 1
    edge = jnp.zeros((8, LANES), jnp.float32)
    moves = [[offs[k, vids[v]] for k in range(slabs)] for v in range(views)]
    for t in range(tiles):
        lanes = pl.ds(t * LANES, LANES)
        for v in range(views):
            grads = pixel_grads(got, absorb_part, emit_part, w, v, t, bands, slabs)
            for k, parts in grads:
                for c in range(channels):
                    shifted[v, k, c, t, 0:8, :] = edge
                    shifted[v, k, c, t, 8 : 8 + rows, :] = parts[c]
                    shifted[v, k, c, t, 8 + rows : 16 + rows, :] = edge
        for k in range(slabs):
            for c in range(channels):

                def total(start):
                    return sum(
                        shifted[v, k, c, t, pl.ds(start + moves[v][k], 4), :]
                        for v in range(views)
                    )

                low, high = total(4), total(8 + rows)
                inner[c, k, :, lanes] = jnp.where(odd, low, high)
                outer[c, k, :, lanes] = jnp.where(odd, high, low)


def main_kernel(offs, vids, got, absorb_part, emit_part, w, main, shifted):
    views, channels, rows, cols = w.shape
    slabs = main.shape[1]
    tiles = cols // LANES
    bands = rows // 8
    edge = jnp.zeros((4, LANES), jnp.float32)
    moves = [[offs[k, vids[v]] for k in range(slabs)] for v in range(views)]
    for t in range(tiles):
        lanes = pl.ds(t * LANES, LANES)
        for v in range(views):
            grads = pixel_grads(got, absorb_part, emit_part, w, v, t, bands, slabs)
            for k, parts in grads:
                for c in range(channels):
                    shifted[v, k, c, t, 4:8, :] = edge
                    shifted[v, k, c, t, 8 : 8 + rows, :] = parts[c]
                    shifted[v, k, c, t, 8 + rows : 12 + rows, :] = edge
        for k in range(slabs):
            for c in range(channels):
                main[c, k, :, lanes] = sum(
                    shifted[v, k, c, t, pl.ds(8 + moves[v][k], rows), :] for v in range(views)
                )


def join_kernel(strip, main, inner, outer, shown, out, image):
    rows = main.shape[2]
    views, channels, _, cols = image.shape
    bands = rows // 8
    odd = lax.rem(strip[0], 2) == 1
    near, far = inner[...], outer[...]
    out[:, :, 0:4, :] = main[:, :, 0:4, :] + jnp.where(odd, near, far)
    out[:, :, 4 : rows - 4, :] = main[:, :, 4 : rows - 4, :]
    out[:, :, rows - 4 :, :] = main[:, :, rows - 4 :, :] + jnp.where(odd, far, near)
    for v in range(views):
        for b in range(bands):
            for t in range(cols // LANES):
                for c in range(channels):
                    image[v, c, 8 * b : 8 * b + 8, t * LANES : (t + 1) * LANES] = shown[
                        v * bands + b, c, t
                    ]


def on_chip(x):
    return pltpu.with_memory_space_constraint(x, pltpu.VMEM)


def on_device(volume, offsets, view_ids, weights):
    channels, slabs, rows, cols = volume.shape
    views = weights.shape[0]
    count = lax.axis_size("depth")
    strips = lax.axis_size("lat")
    tiles, bands = cols // LANES, rows // 8
    depth_total = slabs * count
    size = views * bands
    near = [[size * g + i for i in range(size)] for g in range(count // size)]
    near = [row[::-1] if g in (1, 2) else row for g, row in enumerate(near)]
    far = [[row[i] for row in near] for i in range(size)]
    pairs = [(i, i ^ 1) for i in range(strips)]
    links = [(i, ((i + 1) ^ 1) - 1) for i in range(1, strips - 1)]
    f32 = lambda *shape: jax.ShapeDtypeStruct(shape, jnp.float32)
    kept = lambda *shape: pltpu.VMEM(shape, jnp.float32)
    table = offsets.T
    place = lax.axis_index("depth").reshape(1).astype(jnp.int32)
    w = on_chip(weights)

    def swap(x, groups):
        return lax.all_to_all(x, "depth", 0, 0, tiled=True, axis_index_groups=groups)

    strip = lax.axis_index("lat").reshape(1).astype(jnp.int32)
    odd = (strip & 1) == 1
    first, last = volume[:, :, :HALO], volume[:, :, rows - HALO :]
    outer = lax.ppermute(jnp.where(odd, last, first), "lat", links)
    inner = lax.ppermute(jnp.where(odd, first, last), "lat", pairs)
    own = pl.pallas_call(
        fill_kernel,
        out_shape=kept(channels, slabs, tiles, rows + 16, LANES),
        in_specs=[VMEM],
        out_specs=VMEM,
        compiler_params=LIMIT,
        name="fill",
    )(on_chip(volume))
    agg, ext = pl.pallas_call(
        lambda *refs: slab_kernel(depth_total, *refs),
        out_shape=(
            kept(size, 4, tiles, 8, LANES),
            kept(channels, slabs, tiles, rows + 16, LANES),
        ),
        in_specs=[SMEM, SMEM, SMEM, VMEM, VMEM, VMEM],
        out_specs=(VMEM, VMEM),
        input_output_aliases={5: 1},
        compiler_params=LIMIT,
        name="slab",
    )(table, view_ids, strip, on_chip(inner), on_chip(outer), on_chip(own))
    agg = swap(agg, near)
    absorb_part, emit_part = pl.pallas_call(
        lambda *refs: local_kernel(depth_total, *refs),
        out_shape=(
            kept(views, slabs, tiles, rows, LANES),
            kept(views, slabs, tiles, rows, LANES),
        ),
        in_specs=[SMEM, SMEM, VMEM, VMEM],
        out_specs=(VMEM, VMEM),
        compiler_params=LIMIT,
        name="local",
    )(table, view_ids, on_chip(ext), w)
    agg, absorb_part = lax.optimization_barrier((agg, absorb_part))
    agg = on_chip(agg)
    grouped = pl.pallas_call(
        group_kernel,
        out_shape=kept(count // size, 4, tiles, 8, LANES),
        in_specs=[SMEM, VMEM],
        out_specs=VMEM,
        compiler_params=LIMIT,
        name="group",
    )(place, agg)
    groups = on_chip(swap(grouped, far))
    sent, shown = pl.pallas_call(
        scan_kernel,
        out_shape=(kept(size, 2, tiles, 8, LANES), kept(size, 4, tiles, 8, LANES)),
        in_specs=[SMEM, VMEM, VMEM, VMEM],
        out_specs=(VMEM, VMEM),
        compiler_params=LIMIT,
        name="scan",
    )(place, agg, groups, w)
    got = on_chip(swap(sent, near))
    shown = swap(shown, near)

    to_inner, to_outer = pl.pallas_call(
        edge_kernel,
        out_shape=(
            kept(channels, slabs, HALO, cols),
            kept(channels, slabs, HALO, cols),
        ),
        in_specs=[SMEM, SMEM, SMEM, VMEM, VMEM, VMEM, VMEM],
        out_specs=(VMEM, VMEM),
        scratch_shapes=[
            pltpu.VMEM((views, slabs, channels, tiles, rows + 16, LANES), jnp.float32)
        ],
        compiler_params=LIMIT,
        name="edge",
    )(table, view_ids, strip, got, on_chip(absorb_part), on_chip(emit_part), w)
    from_outer = lax.ppermute(to_outer, "lat", links)
    from_inner = lax.ppermute(to_inner, "lat", pairs)
    main = pl.pallas_call(
        main_kernel,
        out_shape=kept(channels, slabs, rows, cols),
        in_specs=[SMEM, SMEM, VMEM, VMEM, VMEM, VMEM],
        out_specs=VMEM,
        scratch_shapes=[
            pltpu.VMEM((views, slabs, channels, tiles, rows + 16, LANES), jnp.float32)
        ],
        compiler_params=LIMIT,
        name="main",
    )(table, view_ids, got, on_chip(absorb_part), on_chip(emit_part), w)
    grad_out, image_out = pl.pallas_call(
        join_kernel,
        out_shape=(f32(channels, slabs, rows, cols), f32(views, channels, rows, cols)),
        in_specs=[SMEM, VMEM, VMEM, VMEM, VMEM],
        out_specs=(VMEM, VMEM),
        compiler_params=LIMIT,
        name="join",
    )(strip, on_chip(main), on_chip(from_inner), on_chip(from_outer), on_chip(shown))
    return (image_out, grad_out)


def solution(mesh):
    in_specs = (P(None, "depth", "lat", None), P(None, "depth"), P(), P(None, None, "lat", None))
    out_specs = (P(None, None, "lat", None), P(None, "depth", "lat", None))
    return jax.shard_map(
        on_device, mesh=mesh, in_specs=in_specs, out_specs=out_specs, check_vma=False
    )
```

```python
import jax
import jax.numpy as jnp
from jax import lax
from jax.experimental import pallas as pl
from jax.experimental.pallas import tpu as pltpu
from jax.sharding import PartitionSpec as P


HALO = 4
LANES = 128
VMEM = pl.BlockSpec(memory_space=pltpu.VMEM)
SMEM = pl.BlockSpec(memory_space=pltpu.SMEM)
LIMIT = pltpu.CompilerParams(vmem_limit_bytes=16 * 1024 * 1024)


def fill_kernel(vol, ext):
    channels, slabs, rows, cols = vol.shape
    for c in range(channels):
        for k in range(slabs):
            for t in range(cols // LANES):
                ext[c, k, t, 8 : 8 + rows, :] = vol[c, k, :, pl.ds(t * LANES, LANES)]


def slab_kernel(depth_total, offs, vids, strip, inner, outer, own, agg, ext):
    del own
    channels, slabs, tiles, rows = ext.shape[:4]
    rows -= 16
    views = vids.shape[0]
    bands = rows // 8
    odd = lax.rem(strip[0], 2) == 1
    for c in range(channels):
        for k in range(slabs):
            for t in range(tiles):
                lanes = pl.ds(t * LANES, LANES)
                near, far = inner[c, k, :, lanes], outer[c, k, :, lanes]
                ext[c, k, t, 4:8, :] = jnp.where(odd, near, far)
                ext[c, k, t, 8 + rows : 12 + rows, :] = jnp.where(odd, far, near)
    for v in range(views):
        starts = [8 - offs[k, vids[v]] for k in range(slabs)]
        for t in range(tiles):
            transmit = jnp.ones((rows, LANES), jnp.float32)
            colour = [jnp.zeros((rows, LANES), jnp.float32) for _ in range(3)]
            for k in range(slabs):
                part = [ext[c, k, t, pl.ds(starts[k], rows), :] for c in range(channels)]
                keep = jnp.exp(part[3] * (-1.0 / depth_total))
                seen = transmit * (1.0 - keep)
                colour = [colour[c] + seen * part[c] for c in range(3)]
                transmit = transmit * keep
            for b in range(bands):
                owner = v * bands + b
                agg[owner, 0, t] = transmit[8 * b : 8 * b + 8]
                for c in range(3):
                    agg[owner, 1 + c, t] = colour[c][8 * b : 8 * b + 8]


def local_kernel(depth_total, offs, vids, ext, w, absorb_part, emit_part):
    channels, slabs, tiles = ext.shape[:3]
    views, _, rows, _ = w.shape
    for v in range(views):
        starts = [8 - offs[k, vids[v]] for k in range(slabs)]
        for t in range(tiles):
            lanes = pl.ds(t * LANES, LANES)
            weight = [w[v, c, :, lanes] for c in range(3)]
            transmit = jnp.ones((rows, LANES), jnp.float32)
            alphas, keeps, glows, fronts = [], [], [], []
            for k in range(slabs):
                part = [ext[c, k, t, pl.ds(starts[k], rows), :] for c in range(channels)]
                keep = jnp.exp(part[3] * (-1.0 / depth_total))
                alpha = 1.0 - keep
                emit_part[v, k, t] = transmit * alpha * float(depth_total)
                glows.append(weight[0] * part[0] + weight[1] * part[1] + weight[2] * part[2])
                alphas.append(alpha)
                keeps.append(keep)
                transmit = transmit * keep
                fronts.append(transmit)
            behind = jnp.zeros((rows, LANES), jnp.float32)
            for k in range(slabs - 1, -1, -1):
                absorb_part[v, k, t] = fronts[k] * (glows[k] - behind)
                behind = alphas[k] * glows[k] + keeps[k] * behind


def seat(place, members):
    mine, member = lax.div(place[0], members), lax.rem(place[0], members)
    turned = mine >= 2
    half = members // 2
    order = [jnp.where(turned, (j + half) % members, j) for j in range(members)]
    return mine, jnp.where(turned, lax.rem(member + half, members), member), order


def group_kernel(place, agg, out):
    members, _, tiles = agg.shape[:3]
    _, _, order = seat(place, members)
    for t in range(tiles):
        transmit = agg[order[0], 0, t]
        colour = [agg[order[0], 1 + c, t] for c in range(3)]
        for j in range(1, members):
            colour = [colour[c] + transmit * agg[order[j], 1 + c, t] for c in range(3)]
            transmit = transmit * agg[order[j], 0, t]
        for n in range(out.shape[0]):
            out[n, 0, t] = transmit
            for c in range(3):
                out[n, 1 + c, t] = colour[c]


def scan_kernel(place, agg, groups, w, out, shown):
    members, _, tiles = agg.shape[:3]
    mine, owner, order = seat(place, members)
    bands = w.shape[2] // 8
    view, band = lax.div(owner, bands), lax.rem(owner, bands)
    rows = pl.ds(pl.multiple_of(8 * band, 8), 8)
    for t in range(tiles):
        lanes = pl.ds(t * LANES, LANES)
        weight = [w[view, c, rows, lanes] for c in range(4)]
        transmit = jnp.ones((8, LANES), jnp.float32)
        colour = [jnp.zeros((8, LANES), jnp.float32) for _ in range(3)]
        front = transmit
        count = groups.shape[0]
        for g in range(count):
            front = jnp.where(mine == g, transmit, front)
            colour = [colour[c] + transmit * groups[g, 1 + c, t] for c in range(3)]
            transmit = transmit * groups[g, 0, t]
        picture = colour + [1.0 - transmit]
        behind = -weight[3]
        enter = behind
        for g in range(count - 1, 0, -1):
            glow = sum(weight[c] * groups[g, 1 + c, t] for c in range(3))
            behind = glow + groups[g, 0, t] * behind
            enter = jnp.where(mine == g - 1, behind, enter)
        fronts = []
        for j in range(members):
            fronts.append(front)
            front = front * agg[order[j], 0, t]
        for j in range(members - 1, -1, -1):
            passed = agg[order[j], 0, t] * enter
            out[order[j], 0, t] = fronts[j]
            out[order[j], 1, t] = fronts[j] * passed
            for c in range(4):
                shown[j, c, t] = picture[c]
            enter = passed + sum(weight[c] * agg[order[j], 1 + c, t] for c in range(3))


def pixel_grads(got, absorb_part, emit_part, w, v, t, bands, slabs):
    lanes = pl.ds(t * LANES, LANES)
    owners = [v * bands + b for b in range(bands)]
    front = jnp.concatenate([got[n, 0, t] for n in owners], axis=0)
    passed = jnp.concatenate([got[n, 1, t] for n in owners], axis=0)
    weight = [front * w[v, c, :, lanes] for c in range(3)]
    for k in range(slabs):
        emit = emit_part[v, k, t]
        parts = [emit * weight[c] for c in range(3)]
        parts.append(front * absorb_part[v, k, t] - passed)
        yield k, parts


def edge_kernel(offs, vids, strip, got, absorb_part, emit_part, w, inner, outer, shifted):
    views, channels, rows, cols = w.shape
    slabs = inner.shape[1]
    tiles = cols // LANES
    bands = rows // 8
    odd = lax.rem(strip[0], 2) == 1
    edge = jnp.zeros((8, LANES), jnp.float32)
    moves = [[offs[k, vids[v]] for k in range(slabs)] for v in range(views)]
    for t in range(tiles):
        lanes = pl.ds(t * LANES, LANES)
        for v in range(views):
            grads = pixel_grads(got, absorb_part, emit_part, w, v, t, bands, slabs)
            for k, parts in grads:
                for c in range(channels):
                    shifted[v, k, c, t, 0:8, :] = edge
                    shifted[v, k, c, t, 8 : 8 + rows, :] = parts[c]
                    shifted[v, k, c, t, 8 + rows : 16 + rows, :] = edge
        for k in range(slabs):
            for c in range(channels):

                def total(start):
                    return sum(
                        shifted[v, k, c, t, pl.ds(start + moves[v][k], 4), :]
                        for v in range(views)
                    )

                low, high = total(4), total(8 + rows)
                inner[c, k, :, lanes] = jnp.where(odd, low, high)
                outer[c, k, :, lanes] = jnp.where(odd, high, low)


def main_kernel(offs, vids, got, absorb_part, emit_part, w, main, shifted):
    views, channels, rows, cols = w.shape
    slabs = main.shape[1]
    tiles = cols // LANES
    bands = rows // 8
    edge = jnp.zeros((4, LANES), jnp.float32)
    moves = [[offs[k, vids[v]] for k in range(slabs)] for v in range(views)]
    for t in range(tiles):
        lanes = pl.ds(t * LANES, LANES)
        for v in range(views):
            grads = pixel_grads(got, absorb_part, emit_part, w, v, t, bands, slabs)
            for k, parts in grads:
                for c in range(channels):
                    shifted[v, k, c, t, 4:8, :] = edge
                    shifted[v, k, c, t, 8 : 8 + rows, :] = parts[c]
                    shifted[v, k, c, t, 8 + rows : 12 + rows, :] = edge
        for k in range(slabs):
            for c in range(channels):
                main[c, k, :, lanes] = sum(
                    shifted[v, k, c, t, pl.ds(8 + moves[v][k], rows), :] for v in range(views)
                )


def join_kernel(strip, main, inner, outer, shown, out, image):
    rows = main.shape[2]
    views, channels, _, cols = image.shape
    bands = rows // 8
    odd = lax.rem(strip[0], 2) == 1
    near, far = inner[...], outer[...]
    out[:, :, 0:4, :] = main[:, :, 0:4, :] + jnp.where(odd, near, far)
    out[:, :, 4 : rows - 4, :] = main[:, :, 4 : rows - 4, :]
    out[:, :, rows - 4 :, :] = main[:, :, rows - 4 :, :] + jnp.where(odd, far, near)
    for v in range(views):
        for b in range(bands):
            for t in range(cols // LANES):
                for c in range(channels):
                    image[v, c, 8 * b : 8 * b + 8, t * LANES : (t + 1) * LANES] = shown[
                        v * bands + b, c, t
                    ]


def on_chip(x):
    return pltpu.with_memory_space_constraint(x, pltpu.VMEM)


def on_device(volume, offsets, view_ids, weights):
    channels, slabs, rows, cols = volume.shape
    views = weights.shape[0]
    count = lax.axis_size("depth")
    strips = lax.axis_size("lat")
    tiles, bands = cols // LANES, rows // 8
    depth_total = slabs * count
    size = views * bands
    near = [[size * g + i for i in range(size)] for g in range(count // size)]
    near = [row[size // 2 :] + row[: size // 2] if g >= 2 else row for g, row in enumerate(near)]
    far = [[row[i] for row in near] for i in range(size)]
    pairs = [(i, i ^ 1) for i in range(strips)]
    links = [(i, ((i + 1) ^ 1) - 1) for i in range(1, strips - 1)]
    f32 = lambda *shape: jax.ShapeDtypeStruct(shape, jnp.float32)
    kept = lambda *shape: pltpu.VMEM(shape, jnp.float32)
    table = offsets.T
    place = lax.axis_index("depth").reshape(1).astype(jnp.int32)
    w = on_chip(weights)

    def swap(x, groups):
        return lax.all_to_all(x, "depth", 0, 0, tiled=True, axis_index_groups=groups)

    strip = lax.axis_index("lat").reshape(1).astype(jnp.int32)
    odd = (strip & 1) == 1
    first, last = volume[:, :, :HALO], volume[:, :, rows - HALO :]
    outer = lax.ppermute(jnp.where(odd, last, first), "lat", links)
    inner = lax.ppermute(jnp.where(odd, first, last), "lat", pairs)
    own = pl.pallas_call(
        fill_kernel,
        out_shape=kept(channels, slabs, tiles, rows + 16, LANES),
        in_specs=[VMEM],
        out_specs=VMEM,
        compiler_params=LIMIT,
        name="fill",
    )(on_chip(volume))
    agg, ext = pl.pallas_call(
        lambda *refs: slab_kernel(depth_total, *refs),
        out_shape=(
            kept(size, 4, tiles, 8, LANES),
            kept(channels, slabs, tiles, rows + 16, LANES),
        ),
        in_specs=[SMEM, SMEM, SMEM, VMEM, VMEM, VMEM],
        out_specs=(VMEM, VMEM),
        input_output_aliases={5: 1},
        compiler_params=LIMIT,
        name="slab",
    )(table, view_ids, strip, on_chip(inner), on_chip(outer), on_chip(own))
    agg = swap(agg, near)
    absorb_part, emit_part = pl.pallas_call(
        lambda *refs: local_kernel(depth_total, *refs),
        out_shape=(
            kept(views, slabs, tiles, rows, LANES),
            kept(views, slabs, tiles, rows, LANES),
        ),
        in_specs=[SMEM, SMEM, VMEM, VMEM],
        out_specs=(VMEM, VMEM),
        compiler_params=LIMIT,
        name="local",
    )(table, view_ids, on_chip(ext), w)
    agg, absorb_part = lax.optimization_barrier((agg, absorb_part))
    agg = on_chip(agg)
    grouped = pl.pallas_call(
        group_kernel,
        out_shape=kept(count // size, 4, tiles, 8, LANES),
        in_specs=[SMEM, VMEM],
        out_specs=VMEM,
        compiler_params=LIMIT,
        name="group",
    )(place, agg)
    groups = on_chip(swap(grouped, far))
    sent, shown = pl.pallas_call(
        scan_kernel,
        out_shape=(kept(size, 2, tiles, 8, LANES), kept(size, 4, tiles, 8, LANES)),
        in_specs=[SMEM, VMEM, VMEM, VMEM],
        out_specs=(VMEM, VMEM),
        compiler_params=LIMIT,
        name="scan",
    )(place, agg, groups, w)
    got = on_chip(swap(sent, near))
    shown = swap(shown, near)

    to_inner, to_outer = pl.pallas_call(
        edge_kernel,
        out_shape=(
            kept(channels, slabs, HALO, cols),
            kept(channels, slabs, HALO, cols),
        ),
        in_specs=[SMEM, SMEM, SMEM, VMEM, VMEM, VMEM, VMEM],
        out_specs=(VMEM, VMEM),
        scratch_shapes=[
            pltpu.VMEM((views, slabs, channels, tiles, rows + 16, LANES), jnp.float32)
        ],
        compiler_params=LIMIT,
        name="edge",
    )(table, view_ids, strip, got, on_chip(absorb_part), on_chip(emit_part), w)
    from_outer = lax.ppermute(to_outer, "lat", links)
    from_inner = lax.ppermute(to_inner, "lat", pairs)
    main = pl.pallas_call(
        main_kernel,
        out_shape=kept(channels, slabs, rows, cols),
        in_specs=[SMEM, SMEM, VMEM, VMEM, VMEM, VMEM],
        out_specs=VMEM,
        scratch_shapes=[
            pltpu.VMEM((views, slabs, channels, tiles, rows + 16, LANES), jnp.float32)
        ],
        compiler_params=LIMIT,
        name="main",
    )(table, view_ids, got, on_chip(absorb_part), on_chip(emit_part), w)
    grad_out, image_out = pl.pallas_call(
        join_kernel,
        out_shape=(f32(channels, slabs, rows, cols), f32(views, channels, rows, cols)),
        in_specs=[SMEM, VMEM, VMEM, VMEM, VMEM],
        out_specs=(VMEM, VMEM),
        compiler_params=LIMIT,
        name="join",
    )(strip, on_chip(main), on_chip(from_inner), on_chip(from_outer), on_chip(shown))
    return (image_out, grad_out)


def solution(mesh):
    in_specs = (P(None, "depth", "lat", None), P(None, "depth"), P(), P(None, None, "lat", None))
    out_specs = (P(None, None, "lat", None), P(None, "depth", "lat", None))
    return jax.shard_map(
        on_device, mesh=mesh, in_specs=in_specs, out_specs=out_specs, check_vma=False
    )
```

```python
import jax
import jax.numpy as jnp
from jax import lax
from jax.experimental import pallas as pl
from jax.experimental.pallas import tpu as pltpu
from jax.sharding import PartitionSpec as P


HALO = 4
LANES = 128
VMEM = pl.BlockSpec(memory_space=pltpu.VMEM)
SMEM = pl.BlockSpec(memory_space=pltpu.SMEM)
LIMIT = pltpu.CompilerParams(vmem_limit_bytes=16 * 1024 * 1024)


def fill_kernel(vol, ext):
    channels, slabs, rows, cols = vol.shape
    for c in range(channels):
        for k in range(slabs):
            for t in range(cols // LANES):
                ext[c, k, t, 8 : 8 + rows, :] = vol[c, k, :, pl.ds(t * LANES, LANES)]


def slab_kernel(depth_total, offs, vids, strip, inner, outer, own, agg, ext):
    del own
    channels, slabs, tiles, rows = ext.shape[:4]
    rows -= 16
    views = vids.shape[0]
    bands = rows // 8
    odd = lax.rem(strip[0], 2) == 1
    for c in range(channels):
        for k in range(slabs):
            for t in range(tiles):
                lanes = pl.ds(t * LANES, LANES)
                near, far = inner[c, k, :, lanes], outer[c, k, :, lanes]
                ext[c, k, t, 4:8, :] = jnp.where(odd, near, far)
                ext[c, k, t, 8 + rows : 12 + rows, :] = jnp.where(odd, far, near)
    for v in range(views):
        starts = [8 - offs[k, vids[v]] for k in range(slabs)]
        for t in range(tiles):
            transmit = jnp.ones((rows, LANES), jnp.float32)
            colour = [jnp.zeros((rows, LANES), jnp.float32) for _ in range(3)]
            for k in range(slabs):
                part = [ext[c, k, t, pl.ds(starts[k], rows), :] for c in range(channels)]
                keep = jnp.exp(part[3] * (-1.0 / depth_total))
                seen = transmit * (1.0 - keep)
                colour = [colour[c] + seen * part[c] for c in range(3)]
                transmit = transmit * keep
            for b in range(bands):
                owner = v * bands + b
                agg[owner, 0, t] = transmit[8 * b : 8 * b + 8]
                for c in range(3):
                    agg[owner, 1 + c, t] = colour[c][8 * b : 8 * b + 8]


def local_kernel(depth_total, offs, vids, ext, w, absorb_part, emit_part):
    channels, slabs, tiles = ext.shape[:3]
    views, _, rows, _ = w.shape
    for v in range(views):
        starts = [8 - offs[k, vids[v]] for k in range(slabs)]
        for t in range(tiles):
            lanes = pl.ds(t * LANES, LANES)
            weight = [w[v, c, :, lanes] for c in range(3)]
            transmit = jnp.ones((rows, LANES), jnp.float32)
            alphas, keeps, glows, fronts = [], [], [], []
            for k in range(slabs):
                part = [ext[c, k, t, pl.ds(starts[k], rows), :] for c in range(channels)]
                keep = jnp.exp(part[3] * (-1.0 / depth_total))
                alpha = 1.0 - keep
                emit_part[v, k, t] = transmit * alpha * float(depth_total)
                glows.append(weight[0] * part[0] + weight[1] * part[1] + weight[2] * part[2])
                alphas.append(alpha)
                keeps.append(keep)
                transmit = transmit * keep
                fronts.append(transmit)
            behind = jnp.zeros((rows, LANES), jnp.float32)
            for k in range(slabs - 1, -1, -1):
                absorb_part[v, k, t] = fronts[k] * (glows[k] - behind)
                behind = alphas[k] * glows[k] + keeps[k] * behind


def seat(place, members):
    mine, member = lax.div(place[0], members), lax.rem(place[0], members)
    turned = mine >= 2
    half = members // 2
    order = [jnp.where(turned, (j + half) % members, j) for j in range(members)]
    return mine, jnp.where(turned, lax.rem(member + half, members), member), order


def group_kernel(place, agg, out):
    members, _, tiles = agg.shape[:3]
    _, _, order = seat(place, members)
    for t in range(tiles):
        transmit = agg[order[0], 0, t]
        colour = [agg[order[0], 1 + c, t] for c in range(3)]
        for j in range(1, members):
            colour = [colour[c] + transmit * agg[order[j], 1 + c, t] for c in range(3)]
            transmit = transmit * agg[order[j], 0, t]
        out[0, t] = transmit
        for c in range(3):
            out[1 + c, t] = colour[c]


def scan_kernel(place, agg, *refs):
    parts, (w, out, shown) = refs[:-3], refs[-3:]
    members, _, tiles = agg.shape[:3]
    mine, owner, order = seat(place, members)
    bands = w.shape[2] // 8
    view, band = lax.div(owner, bands), lax.rem(owner, bands)
    rows = pl.ds(pl.multiple_of(8 * band, 8), 8)
    for t in range(tiles):
        lanes = pl.ds(t * LANES, LANES)
        weight = [w[view, c, rows, lanes] for c in range(4)]
        transmit = jnp.ones((8, LANES), jnp.float32)
        colour = [jnp.zeros((8, LANES), jnp.float32) for _ in range(3)]
        front = transmit
        count = len(parts)
        own = [[part[c, t] for c in range(4)] for part in parts]
        groups = []
        for g in range(count):
            found = own[g]
            for h in range(1, count):
                found = [jnp.where(mine == h, own[g ^ h][c], found[c]) for c in range(4)]
            groups.append(found)
        for g in range(count):
            front = jnp.where(mine == g, transmit, front)
            colour = [colour[c] + transmit * groups[g][1 + c] for c in range(3)]
            transmit = transmit * groups[g][0]
        picture = colour + [1.0 - transmit]
        behind = -weight[3]
        enter = behind
        for g in range(count - 1, 0, -1):
            glow = sum(weight[c] * groups[g][1 + c] for c in range(3))
            behind = glow + groups[g][0] * behind
            enter = jnp.where(mine == g - 1, behind, enter)
        fronts = []
        for j in range(members):
            fronts.append(front)
            front = front * agg[order[j], 0, t]
        for j in range(members - 1, -1, -1):
            passed = agg[order[j], 0, t] * enter
            out[order[j], 0, t] = fronts[j]
            out[order[j], 1, t] = fronts[j] * passed
            for c in range(4):
                shown[j, c, t] = picture[c]
            enter = passed + sum(weight[c] * agg[order[j], 1 + c, t] for c in range(3))


def pixel_grads(got, absorb_part, emit_part, w, v, t, bands, slabs):
    lanes = pl.ds(t * LANES, LANES)
    owners = [v * bands + b for b in range(bands)]
    front = jnp.concatenate([got[n, 0, t] for n in owners], axis=0)
    passed = jnp.concatenate([got[n, 1, t] for n in owners], axis=0)
    weight = [front * w[v, c, :, lanes] for c in range(3)]
    for k in range(slabs):
        emit = emit_part[v, k, t]
        parts = [emit * weight[c] for c in range(3)]
        parts.append(front * absorb_part[v, k, t] - passed)
        yield k, parts


def edge_kernel(offs, vids, strip, got, absorb_part, emit_part, w, inner, outer, shifted):
    views, channels, rows, cols = w.shape
    slabs = inner.shape[1]
    tiles = cols // LANES
    bands = rows // 8
    odd = lax.rem(strip[0], 2) == 1
    edge = jnp.zeros((8, LANES), jnp.float32)
    moves = [[offs[k, vids[v]] for k in range(slabs)] for v in range(views)]
    for t in range(tiles):
        lanes = pl.ds(t * LANES, LANES)
        for v in range(views):
            grads = pixel_grads(got, absorb_part, emit_part, w, v, t, bands, slabs)
            for k, parts in grads:
                for c in range(channels):
                    shifted[v, k, c, t, 0:8, :] = edge
                    shifted[v, k, c, t, 8 : 8 + rows, :] = parts[c]
                    shifted[v, k, c, t, 8 + rows : 16 + rows, :] = edge
        for k in range(slabs):
            for c in range(channels):

                def total(start):
                    return sum(
                        shifted[v, k, c, t, pl.ds(start + moves[v][k], 4), :]
                        for v in range(views)
                    )

                low, high = total(4), total(8 + rows)
                inner[c, k, :, lanes] = jnp.where(odd, low, high)
                outer[c, k, :, lanes] = jnp.where(odd, high, low)


def main_kernel(offs, vids, got, absorb_part, emit_part, w, main, shifted):
    views, channels, rows, cols = w.shape
    slabs = main.shape[1]
    tiles = cols // LANES
    bands = rows // 8
    edge = jnp.zeros((4, LANES), jnp.float32)
    moves = [[offs[k, vids[v]] for k in range(slabs)] for v in range(views)]
    for t in range(tiles):
        lanes = pl.ds(t * LANES, LANES)
        for v in range(views):
            grads = pixel_grads(got, absorb_part, emit_part, w, v, t, bands, slabs)
            for k, parts in grads:
                for c in range(channels):
                    shifted[v, k, c, t, 4:8, :] = edge
                    shifted[v, k, c, t, 8 : 8 + rows, :] = parts[c]
                    shifted[v, k, c, t, 8 + rows : 12 + rows, :] = edge
        for k in range(slabs):
            for c in range(channels):
                main[c, k, :, lanes] = sum(
                    shifted[v, k, c, t, pl.ds(8 + moves[v][k], rows), :] for v in range(views)
                )


def join_kernel(strip, main, inner, outer, shown, out, image):
    rows = main.shape[2]
    views, channels, _, cols = image.shape
    bands = rows // 8
    odd = lax.rem(strip[0], 2) == 1
    near, far = inner[...], outer[...]
    out[:, :, 0:4, :] = main[:, :, 0:4, :] + jnp.where(odd, near, far)
    out[:, :, 4 : rows - 4, :] = main[:, :, 4 : rows - 4, :]
    out[:, :, rows - 4 :, :] = main[:, :, rows - 4 :, :] + jnp.where(odd, far, near)
    for v in range(views):
        for b in range(bands):
            for t in range(cols // LANES):
                for c in range(channels):
                    image[v, c, 8 * b : 8 * b + 8, t * LANES : (t + 1) * LANES] = shown[
                        v * bands + b, c, t
                    ]


def on_chip(x):
    return pltpu.with_memory_space_constraint(x, pltpu.VMEM)


def on_device(volume, offsets, view_ids, weights):
    channels, slabs, rows, cols = volume.shape
    views = weights.shape[0]
    count = lax.axis_size("depth")
    strips = lax.axis_size("lat")
    tiles, bands = cols // LANES, rows // 8
    depth_total = slabs * count
    size = views * bands
    near = [[size * g + i for i in range(size)] for g in range(count // size)]
    near = [row[size // 2 :] + row[: size // 2] if g >= 2 else row for g, row in enumerate(near)]
    pairs = [(i, i ^ 1) for i in range(strips)]
    links = [(i, ((i + 1) ^ 1) - 1) for i in range(1, strips - 1)]
    f32 = lambda *shape: jax.ShapeDtypeStruct(shape, jnp.float32)
    kept = lambda *shape: pltpu.VMEM(shape, jnp.float32)
    table = offsets.T
    place = lax.axis_index("depth").reshape(1).astype(jnp.int32)
    w = on_chip(weights)

    def swap(x, groups):
        return lax.all_to_all(x, "depth", 0, 0, tiled=True, axis_index_groups=groups)

    strip = lax.axis_index("lat").reshape(1).astype(jnp.int32)
    odd = (strip & 1) == 1
    first, last = volume[:, :, :HALO], volume[:, :, rows - HALO :]
    outer = lax.ppermute(jnp.where(odd, last, first), "lat", links)
    inner = lax.ppermute(jnp.where(odd, first, last), "lat", pairs)
    own = pl.pallas_call(
        fill_kernel,
        out_shape=kept(channels, slabs, tiles, rows + 16, LANES),
        in_specs=[VMEM],
        out_specs=VMEM,
        compiler_params=LIMIT,
        name="fill",
    )(on_chip(volume))
    agg, ext = pl.pallas_call(
        lambda *refs: slab_kernel(depth_total, *refs),
        out_shape=(
            kept(size, 4, tiles, 8, LANES),
            kept(channels, slabs, tiles, rows + 16, LANES),
        ),
        in_specs=[SMEM, SMEM, SMEM, VMEM, VMEM, VMEM],
        out_specs=(VMEM, VMEM),
        input_output_aliases={5: 1},
        compiler_params=LIMIT,
        name="slab",
    )(table, view_ids, strip, on_chip(inner), on_chip(outer), on_chip(own))
    agg = swap(agg, near)
    absorb_part, emit_part = pl.pallas_call(
        lambda *refs: local_kernel(depth_total, *refs),
        out_shape=(
            kept(views, slabs, tiles, rows, LANES),
            kept(views, slabs, tiles, rows, LANES),
        ),
        in_specs=[SMEM, SMEM, VMEM, VMEM],
        out_specs=(VMEM, VMEM),
        compiler_params=LIMIT,
        name="local",
    )(table, view_ids, on_chip(ext), w)
    agg, absorb_part = lax.optimization_barrier((agg, absorb_part))
    agg = on_chip(agg)
    grouped = pl.pallas_call(
        group_kernel,
        out_shape=kept(4, tiles, 8, LANES),
        in_specs=[SMEM, VMEM],
        out_specs=VMEM,
        compiler_params=LIMIT,
        name="group",
    )(place, agg)
    parts = {0: grouped}
    for j in (2, 3, 1):
        hops = [(a, b) for g, row in enumerate(near) for a, b in zip(row, near[g ^ j])]
        parts[j] = lax.ppermute(grouped, "depth", hops)
    parts = [on_chip(parts[j]) for j in range(count // size)]
    sent, shown = pl.pallas_call(
        scan_kernel,
        out_shape=(kept(size, 2, tiles, 8, LANES), kept(size, 4, tiles, 8, LANES)),
        in_specs=[SMEM] + [VMEM] * (2 + count // size),
        out_specs=(VMEM, VMEM),
        compiler_params=LIMIT,
        name="scan",
    )(place, agg, *parts, w)
    got = on_chip(swap(sent, near))
    shown = swap(shown, near)

    to_inner, to_outer = pl.pallas_call(
        edge_kernel,
        out_shape=(
            kept(channels, slabs, HALO, cols),
            kept(channels, slabs, HALO, cols),
        ),
        in_specs=[SMEM, SMEM, SMEM, VMEM, VMEM, VMEM, VMEM],
        out_specs=(VMEM, VMEM),
        scratch_shapes=[
            pltpu.VMEM((views, slabs, channels, tiles, rows + 16, LANES), jnp.float32)
        ],
        compiler_params=LIMIT,
        name="edge",
    )(table, view_ids, strip, got, on_chip(absorb_part), on_chip(emit_part), w)
    from_outer = lax.ppermute(to_outer, "lat", links)
    from_inner = lax.ppermute(to_inner, "lat", pairs)
    main = pl.pallas_call(
        main_kernel,
        out_shape=kept(channels, slabs, rows, cols),
        in_specs=[SMEM, SMEM, VMEM, VMEM, VMEM, VMEM],
        out_specs=VMEM,
        scratch_shapes=[
            pltpu.VMEM((views, slabs, channels, tiles, rows + 16, LANES), jnp.float32)
        ],
        compiler_params=LIMIT,
        name="main",
    )(table, view_ids, got, on_chip(absorb_part), on_chip(emit_part), w)
    grad_out, image_out = pl.pallas_call(
        join_kernel,
        out_shape=(f32(channels, slabs, rows, cols), f32(views, channels, rows, cols)),
        in_specs=[SMEM, VMEM, VMEM, VMEM, VMEM],
        out_specs=(VMEM, VMEM),
        compiler_params=LIMIT,
        name="join",
    )(strip, on_chip(main), on_chip(from_inner), on_chip(from_outer), on_chip(shown))
    return (image_out, grad_out)


def solution(mesh):
    in_specs = (P(None, "depth", "lat", None), P(None, "depth"), P(), P(None, None, "lat", None))
    out_specs = (P(None, None, "lat", None), P(None, "depth", "lat", None))
    return jax.shard_map(
        on_device, mesh=mesh, in_specs=in_specs, out_specs=out_specs, check_vma=False
    )
```

```python
import jax
import jax.numpy as jnp
from jax import lax
from jax.experimental import pallas as pl
from jax.experimental.pallas import tpu as pltpu
from jax.sharding import PartitionSpec as P


HALO = 4
LANES = 128
VMEM = pl.BlockSpec(memory_space=pltpu.VMEM)
SMEM = pl.BlockSpec(memory_space=pltpu.SMEM)
LIMIT = pltpu.CompilerParams(vmem_limit_bytes=16 * 1024 * 1024)


def fill_kernel(vol, ext):
    channels, slabs, rows, cols = vol.shape
    for c in range(channels):
        for k in range(slabs):
            for t in range(cols // LANES):
                ext[c, k, t, 8 : 8 + rows, :] = vol[c, k, :, pl.ds(t * LANES, LANES)]


def slab_kernel(
    depth_total, offs, vids, strip, place, inner, outer, own, w, agg, ext, absorb_part, emit_part
):
    del place, own
    channels, slabs, tiles, rows = ext.shape[:4]
    rows -= 16
    views = vids.shape[0]
    bands = rows // 8
    odd = lax.rem(strip[0], 2) == 1
    for c in range(channels):
        for k in range(slabs):
            for t in range(tiles):
                lanes = pl.ds(t * LANES, LANES)
                near, far = inner[c, k, :, lanes], outer[c, k, :, lanes]
                ext[c, k, t, 4:8, :] = jnp.where(odd, near, far)
                ext[c, k, t, 8 + rows : 12 + rows, :] = jnp.where(odd, far, near)
    for v in range(views):
        starts = [8 - offs[k, vids[v]] for k in range(slabs)]
        for t in range(tiles):
            lanes = pl.ds(t * LANES, LANES)
            weight = [w[v, c, :, lanes] for c in range(3)]
            transmit = jnp.ones((rows, LANES), jnp.float32)
            colour = [jnp.zeros((rows, LANES), jnp.float32) for _ in range(3)]
            alphas, keeps, glows, fronts = [], [], [], []
            for k in range(slabs):
                part = [ext[c, k, t, pl.ds(starts[k], rows), :] for c in range(channels)]
                keep = jnp.exp(part[3] * (-1.0 / depth_total))
                alpha = 1.0 - keep
                seen = transmit * alpha
                colour = [colour[c] + seen * part[c] for c in range(3)]
                emit_part[v, k, t] = seen * float(depth_total)
                glows.append(weight[0] * part[0] + weight[1] * part[1] + weight[2] * part[2])
                alphas.append(alpha)
                keeps.append(keep)
                transmit = transmit * keep
                fronts.append(transmit)
            behind = jnp.zeros((rows, LANES), jnp.float32)
            for k in range(slabs - 1, -1, -1):
                absorb_part[v, k, t] = fronts[k] * (glows[k] - behind)
                behind = alphas[k] * glows[k] + keeps[k] * behind
            for b in range(bands):
                owner = v * bands + b
                agg[owner, 0, t] = transmit[8 * b : 8 * b + 8]
                for c in range(3):
                    agg[owner, 1 + c, t] = colour[c][8 * b : 8 * b + 8]


def seat(place, members):
    mine, member = lax.div(place[0], members), lax.rem(place[0], members)
    turned = mine >= 2
    half = members // 2
    order = [jnp.where(turned, (j + half) % members, j) for j in range(members)]
    return mine, jnp.where(turned, lax.rem(member + half, members), member), order


def group_kernel(place, agg, out):
    members, _, tiles = agg.shape[:3]
    _, _, order = seat(place, members)
    for t in range(tiles):
        transmit = agg[order[0], 0, t]
        colour = [agg[order[0], 1 + c, t] for c in range(3)]
        for j in range(1, members):
            colour = [colour[c] + transmit * agg[order[j], 1 + c, t] for c in range(3)]
            transmit = transmit * agg[order[j], 0, t]
        out[0, t] = transmit
        for c in range(3):
            out[1 + c, t] = colour[c]


def scan_kernel(place, agg, *refs):
    parts, (w, out, shown) = refs[:-3], refs[-3:]
    members, _, tiles = agg.shape[:3]
    mine, owner, order = seat(place, members)
    bands = w.shape[2] // 8
    view, band = lax.div(owner, bands), lax.rem(owner, bands)
    rows = pl.ds(pl.multiple_of(8 * band, 8), 8)
    for t in range(tiles):
        lanes = pl.ds(t * LANES, LANES)
        weight = [w[view, c, rows, lanes] for c in range(4)]
        transmit = jnp.ones((8, LANES), jnp.float32)
        colour = [jnp.zeros((8, LANES), jnp.float32) for _ in range(3)]
        front = transmit
        count = len(parts)
        own = [[part[c, t] for c in range(4)] for part in parts]
        groups = []
        for g in range(count):
            found = own[g]
            for h in range(1, count):
                found = [jnp.where(mine == h, own[g ^ h][c], found[c]) for c in range(4)]
            groups.append(found)
        for g in range(count):
            front = jnp.where(mine == g, transmit, front)
            colour = [colour[c] + transmit * groups[g][1 + c] for c in range(3)]
            transmit = transmit * groups[g][0]
        picture = colour + [1.0 - transmit]
        behind = -weight[3]
        enter = behind
        for g in range(count - 1, 0, -1):
            glow = sum(weight[c] * groups[g][1 + c] for c in range(3))
            behind = glow + groups[g][0] * behind
            enter = jnp.where(mine == g - 1, behind, enter)
        fronts = []
        for j in range(members):
            fronts.append(front)
            front = front * agg[order[j], 0, t]
        for j in range(members - 1, -1, -1):
            passed = agg[order[j], 0, t] * enter
            out[order[j], 0, t] = fronts[j]
            out[order[j], 1, t] = fronts[j] * passed
            for c in range(4):
                shown[j, c, t] = picture[c]
            enter = passed + sum(weight[c] * agg[order[j], 1 + c, t] for c in range(3))


def pixel_grads(got, absorb_part, emit_part, w, v, t, bands, slabs):
    lanes = pl.ds(t * LANES, LANES)
    owners = [v * bands + b for b in range(bands)]
    front = jnp.concatenate([got[n, 0, t] for n in owners], axis=0)
    passed = jnp.concatenate([got[n, 1, t] for n in owners], axis=0)
    weight = [front * w[v, c, :, lanes] for c in range(3)]
    for k in range(slabs):
        emit = emit_part[v, k, t]
        parts = [emit * weight[c] for c in range(3)]
        parts.append(front * absorb_part[v, k, t] - passed)
        yield k, parts


def edge_kernel(offs, vids, strip, got, absorb_part, emit_part, w, inner, outer, shifted):
    views, channels, rows, cols = w.shape
    slabs = inner.shape[1]
    tiles = cols // LANES
    bands = rows // 8
    odd = lax.rem(strip[0], 2) == 1
    edge = jnp.zeros((8, LANES), jnp.float32)
    moves = [[offs[k, vids[v]] for k in range(slabs)] for v in range(views)]
    for t in range(tiles):
        lanes = pl.ds(t * LANES, LANES)
        for v in range(views):
            grads = pixel_grads(got, absorb_part, emit_part, w, v, t, bands, slabs)
            for k, parts in grads:
                for c in range(channels):
                    shifted[v, k, c, t, 0:8, :] = edge
                    shifted[v, k, c, t, 8 : 8 + rows, :] = parts[c]
                    shifted[v, k, c, t, 8 + rows : 16 + rows, :] = edge
        for k in range(slabs):
            for c in range(channels):

                def total(start):
                    return sum(
                        shifted[v, k, c, t, pl.ds(start + moves[v][k], 4), :]
                        for v in range(views)
                    )

                low, high = total(4), total(8 + rows)
                inner[c, k, :, lanes] = jnp.where(odd, low, high)
                outer[c, k, :, lanes] = jnp.where(odd, high, low)


def main_kernel(offs, vids, got, absorb_part, emit_part, w, main, shifted):
    views, channels, rows, cols = w.shape
    slabs = main.shape[1]
    tiles = cols // LANES
    bands = rows // 8
    edge = jnp.zeros((4, LANES), jnp.float32)
    moves = [[offs[k, vids[v]] for k in range(slabs)] for v in range(views)]
    for t in range(tiles):
        lanes = pl.ds(t * LANES, LANES)
        for v in range(views):
            grads = pixel_grads(got, absorb_part, emit_part, w, v, t, bands, slabs)
            for k, parts in grads:
                for c in range(channels):
                    shifted[v, k, c, t, 4:8, :] = edge
                    shifted[v, k, c, t, 8 : 8 + rows, :] = parts[c]
                    shifted[v, k, c, t, 8 + rows : 12 + rows, :] = edge
        for k in range(slabs):
            for c in range(channels):
                main[c, k, :, lanes] = sum(
                    shifted[v, k, c, t, pl.ds(8 + moves[v][k], rows), :] for v in range(views)
                )


def join_kernel(strip, main, inner, outer, shown, out, image):
    rows = main.shape[2]
    views, channels, _, cols = image.shape
    bands = rows // 8
    odd = lax.rem(strip[0], 2) == 1
    near, far = inner[...], outer[...]
    out[:, :, 0:4, :] = main[:, :, 0:4, :] + jnp.where(odd, near, far)
    out[:, :, 4 : rows - 4, :] = main[:, :, 4 : rows - 4, :]
    out[:, :, rows - 4 :, :] = main[:, :, rows - 4 :, :] + jnp.where(odd, far, near)
    for v in range(views):
        for b in range(bands):
            for t in range(cols // LANES):
                for c in range(channels):
                    image[v, c, 8 * b : 8 * b + 8, t * LANES : (t + 1) * LANES] = shown[
                        v * bands + b, c, t
                    ]


def off_chip(x):
    return pltpu.with_memory_space_constraint(x, pltpu.HBM)


def on_chip(x):
    return pltpu.with_memory_space_constraint(x, pltpu.VMEM)


def on_device(volume, offsets, view_ids, weights):
    channels, slabs, rows, cols = volume.shape
    views = weights.shape[0]
    count = lax.axis_size("depth")
    strips = lax.axis_size("lat")
    tiles, bands = cols // LANES, rows // 8
    depth_total = slabs * count
    size = views * bands
    near = [[size * g + i for i in range(size)] for g in range(count // size)]
    near = [row[size // 2 :] + row[: size // 2] if g >= 2 else row for g, row in enumerate(near)]
    pairs = [(i, i ^ 1) for i in range(strips)]
    links = [(i, ((i + 1) ^ 1) - 1) for i in range(1, strips - 1)]
    f32 = lambda *shape: jax.ShapeDtypeStruct(shape, jnp.float32)
    kept = lambda *shape: pltpu.VMEM(shape, jnp.float32)
    table, view_ids = off_chip(offsets.T), off_chip(view_ids)
    place = lax.axis_index("depth").reshape(1).astype(jnp.int32)
    w = on_chip(weights)

    def swap(x, groups):
        return lax.all_to_all(x, "depth", 0, 0, tiled=True, axis_index_groups=groups)

    strip = lax.axis_index("lat").reshape(1).astype(jnp.int32)
    odd = (strip & 1) == 1
    first, last = volume[:, :, :HALO], volume[:, :, rows - HALO :]
    outer = lax.ppermute(jnp.where(odd, last, first), "lat", links)
    inner = lax.ppermute(jnp.where(odd, first, last), "lat", pairs)
    own = pl.pallas_call(
        fill_kernel,
        out_shape=kept(channels, slabs, tiles, rows + 16, LANES),
        in_specs=[VMEM],
        out_specs=VMEM,
        compiler_params=LIMIT,
        name="fill",
    )(on_chip(volume))
    agg, _, absorb_part, emit_part = pl.pallas_call(
        lambda *refs: slab_kernel(depth_total, *refs),
        out_shape=(
            kept(size, 4, tiles, 8, LANES),
            kept(channels, slabs, tiles, rows + 16, LANES),
            kept(views, slabs, tiles, rows, LANES),
            kept(views, slabs, tiles, rows, LANES),
        ),
        in_specs=[SMEM, SMEM, SMEM, SMEM, VMEM, VMEM, VMEM, VMEM],
        out_specs=(VMEM, VMEM, VMEM, VMEM),
        input_output_aliases={6: 1},
        compiler_params=LIMIT,
        name="slab",
    )(table, view_ids, strip, place, on_chip(inner), on_chip(outer), on_chip(own), w)
    agg = on_chip(swap(agg, near))
    grouped = pl.pallas_call(
        group_kernel,
        out_shape=kept(4, tiles, 8, LANES),
        in_specs=[SMEM, VMEM],
        out_specs=VMEM,
        compiler_params=LIMIT,
        name="group",
    )(place, agg)
    parts = {0: grouped}
    for j in (2, 3, 1):
        hops = [(a, b) for g, row in enumerate(near) for a, b in zip(row, near[g ^ j])]
        parts[j] = lax.ppermute(grouped, "depth", hops)
    parts = [on_chip(parts[j]) for j in range(count // size)]
    sent, shown = pl.pallas_call(
        scan_kernel,
        out_shape=(kept(size, 2, tiles, 8, LANES), kept(size, 4, tiles, 8, LANES)),
        in_specs=[SMEM] + [VMEM] * (2 + count // size),
        out_specs=(VMEM, VMEM),
        compiler_params=LIMIT,
        name="scan",
    )(place, agg, *parts, w)
    got = on_chip(swap(sent, near))
    shown = swap(shown, near)

    to_inner, to_outer = pl.pallas_call(
        edge_kernel,
        out_shape=(
            kept(channels, slabs, HALO, cols),
            kept(channels, slabs, HALO, cols),
        ),
        in_specs=[SMEM, SMEM, SMEM, VMEM, VMEM, VMEM, VMEM],
        out_specs=(VMEM, VMEM),
        scratch_shapes=[
            pltpu.VMEM((views, slabs, channels, tiles, rows + 16, LANES), jnp.float32)
        ],
        compiler_params=LIMIT,
        name="edge",
    )(table, view_ids, strip, got, on_chip(absorb_part), on_chip(emit_part), w)
    from_outer = lax.ppermute(to_outer, "lat", links)
    from_inner = lax.ppermute(to_inner, "lat", pairs)
    main = pl.pallas_call(
        main_kernel,
        out_shape=kept(channels, slabs, rows, cols),
        in_specs=[SMEM, SMEM, VMEM, VMEM, VMEM, VMEM],
        out_specs=VMEM,
        scratch_shapes=[
            pltpu.VMEM((views, slabs, channels, tiles, rows + 16, LANES), jnp.float32)
        ],
        compiler_params=LIMIT,
        name="main",
    )(table, view_ids, got, on_chip(absorb_part), on_chip(emit_part), w)
    grad_out, image_out = pl.pallas_call(
        join_kernel,
        out_shape=(f32(channels, slabs, rows, cols), f32(views, channels, rows, cols)),
        in_specs=[SMEM, VMEM, VMEM, VMEM, VMEM],
        out_specs=(VMEM, VMEM),
        compiler_params=LIMIT,
        name="join",
    )(strip, on_chip(main), on_chip(from_inner), on_chip(from_outer), on_chip(shown))
    return (image_out, grad_out)


def solution(mesh):
    in_specs = (P(None, "depth", "lat", None), P(None, "depth"), P(), P(None, None, "lat", None))
    out_specs = (P(None, None, "lat", None), P(None, "depth", "lat", None))
    return jax.shard_map(
        on_device, mesh=mesh, in_specs=in_specs, out_specs=out_specs, check_vma=False
    )
```

```python
import jax
import jax.numpy as jnp
from jax import lax
from jax.experimental import pallas as pl
from jax.experimental.pallas import tpu as pltpu
from jax.sharding import PartitionSpec as P


HALO = 4
LANES = 128
VMEM = pl.BlockSpec(memory_space=pltpu.VMEM)
SMEM = pl.BlockSpec(memory_space=pltpu.SMEM)
LIMIT = pltpu.CompilerParams(vmem_limit_bytes=16 * 1024 * 1024)


def fill_kernel(vol, ext):
    channels, slabs, rows, cols = vol.shape
    for c in range(channels):
        for k in range(slabs):
            for t in range(cols // LANES):
                ext[c, k, t, 8 : 8 + rows, :] = vol[c, k, :, pl.ds(t * LANES, LANES)]


def slab_kernel(
    depth_total, offs, vids, strip, place, inner, outer, own, w, agg, ext, absorb_part, emit_part
):
    del place, own
    channels, slabs, tiles, rows = ext.shape[:4]
    rows -= 16
    views = vids.shape[0]
    bands = rows // 8
    odd = lax.rem(strip[0], 2) == 1
    for c in range(channels):
        for k in range(slabs):
            for t in range(tiles):
                lanes = pl.ds(t * LANES, LANES)
                near, far = inner[c, k, :, lanes], outer[c, k, :, lanes]
                ext[c, k, t, 4:8, :] = jnp.where(odd, near, far)
                ext[c, k, t, 8 + rows : 12 + rows, :] = jnp.where(odd, far, near)
    for v in range(views):
        starts = [8 - offs[k, vids[v]] for k in range(slabs)]
        for t in range(tiles):
            lanes = pl.ds(t * LANES, LANES)
            weight = [w[v, c, :, lanes] for c in range(3)]
            transmit = jnp.ones((rows, LANES), jnp.float32)
            colour = [jnp.zeros((rows, LANES), jnp.float32) for _ in range(3)]
            alphas, keeps, glows, fronts = [], [], [], []
            for k in range(slabs):
                part = [ext[c, k, t, pl.ds(starts[k], rows), :] for c in range(channels)]
                keep = jnp.exp(part[3] * (-1.0 / depth_total))
                alpha = 1.0 - keep
                seen = transmit * alpha
                colour = [colour[c] + seen * part[c] for c in range(3)]
                emit_part[v, k, t] = seen * float(depth_total)
                glows.append(weight[0] * part[0] + weight[1] * part[1] + weight[2] * part[2])
                alphas.append(alpha)
                keeps.append(keep)
                transmit = transmit * keep
                fronts.append(transmit)
            behind = jnp.zeros((rows, LANES), jnp.float32)
            for k in range(slabs - 1, -1, -1):
                absorb_part[v, k, t] = fronts[k] * (glows[k] - behind)
                behind = alphas[k] * glows[k] + keeps[k] * behind
            for b in range(bands):
                owner = v * bands + b
                agg[owner, 0, t] = transmit[8 * b : 8 * b + 8]
                for c in range(3):
                    agg[owner, 1 + c, t] = colour[c][8 * b : 8 * b + 8]


def seat(place, members):
    mine, member = lax.div(place[0], members), lax.rem(place[0], members)
    turned = mine >= 2
    half = members // 2
    order = [jnp.where(turned, (j + half) % members, j) for j in range(members)]
    return mine, jnp.where(turned, lax.rem(member + half, members), member), order


def group_kernel(place, agg, out):
    members, _, tiles = agg.shape[:3]
    _, _, order = seat(place, members)
    for t in range(tiles):
        transmit = agg[order[0], 0, t]
        colour = [agg[order[0], 1 + c, t] for c in range(3)]
        for j in range(1, members):
            colour = [colour[c] + transmit * agg[order[j], 1 + c, t] for c in range(3)]
            transmit = transmit * agg[order[j], 0, t]
        out[0, t] = transmit
        for c in range(3):
            out[1 + c, t] = colour[c]


def scan_kernel(place, agg, *refs):
    parts, (w, out) = refs[:-2], refs[-2:]
    members, _, tiles = agg.shape[:3]
    mine, owner, order = seat(place, members)
    bands = w.shape[2] // 8
    view, band = lax.div(owner, bands), lax.rem(owner, bands)
    rows = pl.ds(pl.multiple_of(8 * band, 8), 8)
    for t in range(tiles):
        lanes = pl.ds(t * LANES, LANES)
        weight = [w[view, c, rows, lanes] for c in range(4)]
        transmit = jnp.ones((8, LANES), jnp.float32)
        colour = [jnp.zeros((8, LANES), jnp.float32) for _ in range(3)]
        front = transmit
        count = len(parts)
        own = [[part[c, t] for c in range(4)] for part in parts]
        groups = []
        for g in range(count):
            found = own[g]
            for h in range(1, count):
                found = [jnp.where(mine == h, own[g ^ h][c], found[c]) for c in range(4)]
            groups.append(found)
        for g in range(count):
            front = jnp.where(mine == g, transmit, front)
            colour = [colour[c] + transmit * groups[g][1 + c] for c in range(3)]
            transmit = transmit * groups[g][0]
        picture = colour + [1.0 - transmit]
        behind = -weight[3]
        enter = behind
        for g in range(count - 1, 0, -1):
            glow = sum(weight[c] * groups[g][1 + c] for c in range(3))
            behind = glow + groups[g][0] * behind
            enter = jnp.where(mine == g - 1, behind, enter)
        fronts = []
        for j in range(members):
            fronts.append(front)
            front = front * agg[order[j], 0, t]
        for j in range(members - 1, -1, -1):
            passed = agg[order[j], 0, t] * enter
            out[order[j], 0, t] = fronts[j]
            out[order[j], 1, t] = fronts[j] * passed
            for c in range(4):
                out[order[j], 2 + c, t] = picture[c]
            enter = passed + sum(weight[c] * agg[order[j], 1 + c, t] for c in range(3))


def pixel_grads(got, absorb_part, emit_part, w, v, t, bands, slabs):
    lanes = pl.ds(t * LANES, LANES)
    owners = [v * bands + b for b in range(bands)]
    front = jnp.concatenate([got[n, 0, t] for n in owners], axis=0)
    passed = jnp.concatenate([got[n, 1, t] for n in owners], axis=0)
    weight = [front * w[v, c, :, lanes] for c in range(3)]
    for k in range(slabs):
        emit = emit_part[v, k, t]
        parts = [emit * weight[c] for c in range(3)]
        parts.append(front * absorb_part[v, k, t] - passed)
        yield k, parts


def edge_kernel(offs, vids, strip, got, absorb_part, emit_part, w, inner, outer, shifted):
    views, channels, rows, cols = w.shape
    slabs = inner.shape[1]
    tiles = cols // LANES
    bands = rows // 8
    odd = lax.rem(strip[0], 2) == 1
    edge = jnp.zeros((8, LANES), jnp.float32)
    moves = [[offs[k, vids[v]] for k in range(slabs)] for v in range(views)]
    for t in range(tiles):
        lanes = pl.ds(t * LANES, LANES)
        for v in range(views):
            grads = pixel_grads(got, absorb_part, emit_part, w, v, t, bands, slabs)
            for k, parts in grads:
                for c in range(channels):
                    shifted[v, k, c, t, 0:8, :] = edge
                    shifted[v, k, c, t, 8 : 8 + rows, :] = parts[c]
                    shifted[v, k, c, t, 8 + rows : 16 + rows, :] = edge
        for k in range(slabs):
            for c in range(channels):

                def total(start):
                    return sum(
                        shifted[v, k, c, t, pl.ds(start + moves[v][k], 4), :]
                        for v in range(views)
                    )

                low, high = total(4), total(8 + rows)
                inner[c, k, :, lanes] = jnp.where(odd, low, high)
                outer[c, k, :, lanes] = jnp.where(odd, high, low)


def main_kernel(offs, vids, got, absorb_part, emit_part, w, main, shifted):
    views, channels, rows, cols = w.shape
    slabs = main.shape[1]
    tiles = cols // LANES
    bands = rows // 8
    edge = jnp.zeros((4, LANES), jnp.float32)
    moves = [[offs[k, vids[v]] for k in range(slabs)] for v in range(views)]
    for t in range(tiles):
        lanes = pl.ds(t * LANES, LANES)
        for v in range(views):
            grads = pixel_grads(got, absorb_part, emit_part, w, v, t, bands, slabs)
            for k, parts in grads:
                for c in range(channels):
                    shifted[v, k, c, t, 4:8, :] = edge
                    shifted[v, k, c, t, 8 : 8 + rows, :] = parts[c]
                    shifted[v, k, c, t, 8 + rows : 12 + rows, :] = edge
        for k in range(slabs):
            for c in range(channels):
                main[c, k, :, lanes] = sum(
                    shifted[v, k, c, t, pl.ds(8 + moves[v][k], rows), :] for v in range(views)
                )


def join_kernel(strip, main, inner, outer, shown, out, image):
    rows = main.shape[2]
    views, channels, _, cols = image.shape
    bands = rows // 8
    odd = lax.rem(strip[0], 2) == 1
    near, far = inner[...], outer[...]
    out[:, :, 0:4, :] = main[:, :, 0:4, :] + jnp.where(odd, near, far)
    out[:, :, 4 : rows - 4, :] = main[:, :, 4 : rows - 4, :]
    out[:, :, rows - 4 :, :] = main[:, :, rows - 4 :, :] + jnp.where(odd, far, near)
    for v in range(views):
        for b in range(bands):
            for t in range(cols // LANES):
                for c in range(channels):
                    image[v, c, 8 * b : 8 * b + 8, t * LANES : (t + 1) * LANES] = shown[
                        v * bands + b, 2 + c, t
                    ]


def off_chip(x):
    return pltpu.with_memory_space_constraint(x, pltpu.HBM)


def on_chip(x):
    return pltpu.with_memory_space_constraint(x, pltpu.VMEM)


def on_device(volume, offsets, view_ids, weights):
    channels, slabs, rows, cols = volume.shape
    views = weights.shape[0]
    count = lax.axis_size("depth")
    strips = lax.axis_size("lat")
    tiles, bands = cols // LANES, rows // 8
    depth_total = slabs * count
    size = views * bands
    near = [[size * g + i for i in range(size)] for g in range(count // size)]
    near = [row[size // 2 :] + row[: size // 2] if g >= 2 else row for g, row in enumerate(near)]
    pairs = [(i, i ^ 1) for i in range(strips)]
    links = [(i, ((i + 1) ^ 1) - 1) for i in range(1, strips - 1)]
    f32 = lambda *shape: jax.ShapeDtypeStruct(shape, jnp.float32)
    kept = lambda *shape: pltpu.VMEM(shape, jnp.float32)
    table, view_ids = off_chip(offsets.T), off_chip(view_ids)
    place = lax.axis_index("depth").reshape(1).astype(jnp.int32)
    w = on_chip(weights)

    def swap(x, groups):
        return lax.all_to_all(x, "depth", 0, 0, tiled=True, axis_index_groups=groups)

    strip = lax.axis_index("lat").reshape(1).astype(jnp.int32)
    odd = (strip & 1) == 1
    first, last = volume[:, :, :HALO], volume[:, :, rows - HALO :]
    outer = lax.ppermute(jnp.where(odd, last, first), "lat", links)
    inner = lax.ppermute(jnp.where(odd, first, last), "lat", pairs)
    own = pl.pallas_call(
        fill_kernel,
        out_shape=kept(channels, slabs, tiles, rows + 16, LANES),
        in_specs=[VMEM],
        out_specs=VMEM,
        compiler_params=LIMIT,
        name="fill",
    )(on_chip(volume))
    agg, _, absorb_part, emit_part = pl.pallas_call(
        lambda *refs: slab_kernel(depth_total, *refs),
        out_shape=(
            kept(size, 4, tiles, 8, LANES),
            kept(channels, slabs, tiles, rows + 16, LANES),
            kept(views, slabs, tiles, rows, LANES),
            kept(views, slabs, tiles, rows, LANES),
        ),
        in_specs=[SMEM, SMEM, SMEM, SMEM, VMEM, VMEM, VMEM, VMEM],
        out_specs=(VMEM, VMEM, VMEM, VMEM),
        input_output_aliases={6: 1},
        compiler_params=LIMIT,
        name="slab",
    )(table, view_ids, strip, place, on_chip(inner), on_chip(outer), on_chip(own), w)
    agg = on_chip(swap(agg, near))
    grouped = pl.pallas_call(
        group_kernel,
        out_shape=kept(4, tiles, 8, LANES),
        in_specs=[SMEM, VMEM],
        out_specs=VMEM,
        compiler_params=LIMIT,
        name="group",
    )(place, agg)
    parts = {0: grouped}
    for j in (2, 3, 1):
        hops = [(a, b) for g, row in enumerate(near) for a, b in zip(row, near[g ^ j])]
        parts[j] = lax.ppermute(grouped, "depth", hops)
    parts = [on_chip(parts[j]) for j in range(count // size)]
    sent = pl.pallas_call(
        scan_kernel,
        out_shape=kept(size, 6, tiles, 8, LANES),
        in_specs=[SMEM] + [VMEM] * (2 + count // size),
        out_specs=VMEM,
        compiler_params=LIMIT,
        name="scan",
    )(place, agg, *parts, w)
    got = on_chip(swap(sent, near))
    shown = got

    to_inner, to_outer = pl.pallas_call(
        edge_kernel,
        out_shape=(
            kept(channels, slabs, HALO, cols),
            kept(channels, slabs, HALO, cols),
        ),
        in_specs=[SMEM, SMEM, SMEM, VMEM, VMEM, VMEM, VMEM],
        out_specs=(VMEM, VMEM),
        scratch_shapes=[
            pltpu.VMEM((views, slabs, channels, tiles, rows + 16, LANES), jnp.float32)
        ],
        compiler_params=LIMIT,
        name="edge",
    )(table, view_ids, strip, got, on_chip(absorb_part), on_chip(emit_part), w)
    from_outer = lax.ppermute(to_outer, "lat", links)
    from_inner = lax.ppermute(to_inner, "lat", pairs)
    main = pl.pallas_call(
        main_kernel,
        out_shape=kept(channels, slabs, rows, cols),
        in_specs=[SMEM, SMEM, VMEM, VMEM, VMEM, VMEM],
        out_specs=VMEM,
        scratch_shapes=[
            pltpu.VMEM((views, slabs, channels, tiles, rows + 16, LANES), jnp.float32)
        ],
        compiler_params=LIMIT,
        name="main",
    )(table, view_ids, got, on_chip(absorb_part), on_chip(emit_part), w)
    grad_out, image_out = pl.pallas_call(
        join_kernel,
        out_shape=(f32(channels, slabs, rows, cols), f32(views, channels, rows, cols)),
        in_specs=[SMEM, VMEM, VMEM, VMEM, VMEM],
        out_specs=(VMEM, VMEM),
        compiler_params=LIMIT,
        name="join",
    )(strip, on_chip(main), on_chip(from_inner), on_chip(from_outer), on_chip(shown))
    return (image_out, grad_out)


def solution(mesh):
    in_specs = (P(None, "depth", "lat", None), P(None, "depth"), P(), P(None, None, "lat", None))
    out_specs = (P(None, None, "lat", None), P(None, "depth", "lat", None))
    return jax.shard_map(
        on_device, mesh=mesh, in_specs=in_specs, out_specs=out_specs, check_vma=False
    )
```

```python
import jax
import jax.numpy as jnp
from jax import lax
from jax.experimental import pallas as pl
from jax.experimental.pallas import tpu as pltpu
from jax.sharding import PartitionSpec as P


HALO = 4
LANES = 128
VMEM = pl.BlockSpec(memory_space=pltpu.VMEM)
SMEM = pl.BlockSpec(memory_space=pltpu.SMEM)
LIMIT = pltpu.CompilerParams(vmem_limit_bytes=16 * 1024 * 1024)


def fill_kernel(vol, ext):
    channels, slabs, rows, cols = vol.shape
    for c in range(channels):
        for k in range(slabs):
            for t in range(cols // LANES):
                ext[c, k, t, 8 : 8 + rows, :] = vol[c, k, :, pl.ds(t * LANES, LANES)]


def slab_kernel(
    depth_total, offs, vids, strip, place, inner, outer, own, w, agg, ext, absorb_part, emit_part
):
    del place, own
    channels, slabs, tiles, rows = ext.shape[:4]
    rows -= 16
    views = vids.shape[0]
    bands = rows // 8
    odd = lax.rem(strip[0], 2) == 1
    for c in range(channels):
        for k in range(slabs):
            for t in range(tiles):
                lanes = pl.ds(t * LANES, LANES)
                near, far = inner[c, k, :, lanes], outer[c, k, :, lanes]
                ext[c, k, t, 4:8, :] = jnp.where(odd, near, far)
                ext[c, k, t, 8 + rows : 12 + rows, :] = jnp.where(odd, far, near)
    for v in range(views):
        starts = [8 - offs[k, vids[v]] for k in range(slabs)]
        for t in range(tiles):
            lanes = pl.ds(t * LANES, LANES)
            weight = [w[v, c, :, lanes] for c in range(3)]
            transmit = jnp.ones((rows, LANES), jnp.float32)
            colour = [jnp.zeros((rows, LANES), jnp.float32) for _ in range(3)]
            alphas, keeps, glows, fronts = [], [], [], []
            for k in range(slabs):
                part = [ext[c, k, t, pl.ds(starts[k], rows), :] for c in range(channels)]
                keep = jnp.exp(part[3] * (-1.0 / depth_total))
                alpha = 1.0 - keep
                seen = transmit * alpha
                colour = [colour[c] + seen * part[c] for c in range(3)]
                emit_part[v, k, t] = seen * float(depth_total)
                glows.append(weight[0] * part[0] + weight[1] * part[1] + weight[2] * part[2])
                alphas.append(alpha)
                keeps.append(keep)
                transmit = transmit * keep
                fronts.append(transmit)
            behind = jnp.zeros((rows, LANES), jnp.float32)
            for k in range(slabs - 1, -1, -1):
                absorb_part[v, k, t] = fronts[k] * (glows[k] - behind)
                behind = alphas[k] * glows[k] + keeps[k] * behind
            for b in range(bands):
                owner = v * bands + b
                agg[owner, 0, t] = transmit[8 * b : 8 * b + 8]
                for c in range(3):
                    agg[owner, 1 + c, t] = colour[c][8 * b : 8 * b + 8]


def seat(place, members):
    mine, member = lax.div(place[0], members), lax.rem(place[0], members)
    turned = mine >= 2
    half = members // 2
    order = [jnp.where(turned, (j + half) % members, j) for j in range(members)]
    return mine, jnp.where(turned, lax.rem(member + half, members), member), order


def group_kernel(place, agg, out):
    members, _, tiles = agg.shape[:3]
    _, _, order = seat(place, members)
    for t in range(tiles):
        transmit = agg[order[0], 0, t]
        colour = [agg[order[0], 1 + c, t] for c in range(3)]
        for j in range(1, members):
            colour = [colour[c] + transmit * agg[order[j], 1 + c, t] for c in range(3)]
            transmit = transmit * agg[order[j], 0, t]
        out[0, t] = transmit
        for c in range(3):
            out[1 + c, t] = colour[c]


def scan_kernel(place, agg, *refs):
    parts, (w, out) = refs[:-2], refs[-2:]
    members, _, tiles = agg.shape[:3]
    mine, owner, order = seat(place, members)
    bands = w.shape[2] // 8
    view, band = lax.div(owner, bands), lax.rem(owner, bands)
    rows = pl.ds(pl.multiple_of(8 * band, 8), 8)
    for t in range(tiles):
        lanes = pl.ds(t * LANES, LANES)
        weight = [w[view, c, rows, lanes] for c in range(4)]
        transmit = jnp.ones((8, LANES), jnp.float32)
        colour = [jnp.zeros((8, LANES), jnp.float32) for _ in range(3)]
        front = transmit
        count = len(parts)
        own = [[part[c, t] for c in range(4)] for part in parts]
        groups = []
        for g in range(count):
            found = own[g]
            for h in range(1, count):
                found = [jnp.where(mine == h, own[g ^ h][c], found[c]) for c in range(4)]
            groups.append(found)
        for g in range(count):
            front = jnp.where(mine == g, transmit, front)
            colour = [colour[c] + transmit * groups[g][1 + c] for c in range(3)]
            transmit = transmit * groups[g][0]
        picture = colour + [1.0 - transmit]
        behind = -weight[3]
        enter = behind
        for g in range(count - 1, 0, -1):
            glow = sum(weight[c] * groups[g][1 + c] for c in range(3))
            behind = glow + groups[g][0] * behind
            enter = jnp.where(mine == g - 1, behind, enter)
        fronts = []
        for j in range(members):
            fronts.append(front)
            front = front * agg[order[j], 0, t]
        for j in range(members - 1, -1, -1):
            passed = agg[order[j], 0, t] * enter
            out[order[j], 0, t] = fronts[j]
            out[order[j], 1, t] = fronts[j] * passed
            for c in range(4):
                out[order[j], 2 + c, t] = picture[c]
            enter = passed + sum(weight[c] * agg[order[j], 1 + c, t] for c in range(3))


def pixel_grads(got, absorb_part, emit_part, w, v, t, bands, slabs):
    lanes = pl.ds(t * LANES, LANES)
    owners = [v * bands + b for b in range(bands)]
    front = jnp.concatenate([got[n, 0, t] for n in owners], axis=0)
    passed = jnp.concatenate([got[n, 1, t] for n in owners], axis=0)
    weight = [front * w[v, c, :, lanes] for c in range(3)]
    for k in range(slabs):
        emit = emit_part[v, k, t]
        parts = [emit * weight[c] for c in range(3)]
        parts.append(front * absorb_part[v, k, t] - passed)
        yield k, parts


def edge_kernel(offs, vids, strip, got, absorb_part, emit_part, w, inner, outer, shifted):
    views, channels, rows, cols = w.shape
    slabs = inner.shape[1]
    tiles = cols // LANES
    bands = rows // 8
    odd = lax.rem(strip[0], 2) == 1
    edge = jnp.zeros((8, LANES), jnp.float32)
    moves = [[offs[k, vids[v]] for k in range(slabs)] for v in range(views)]
    for t in range(tiles):
        lanes = pl.ds(t * LANES, LANES)
        for v in range(views):
            grads = pixel_grads(got, absorb_part, emit_part, w, v, t, bands, slabs)
            for k, parts in grads:
                for c in range(channels):
                    shifted[v, k, c, t, 0:8, :] = edge
                    shifted[v, k, c, t, 8 : 8 + rows, :] = parts[c]
                    shifted[v, k, c, t, 8 + rows : 16 + rows, :] = edge
        for k in range(slabs):
            for c in range(channels):

                def total(start):
                    return sum(
                        shifted[v, k, c, t, pl.ds(start + moves[v][k], 4), :]
                        for v in range(views)
                    )

                low, high = total(4), total(8 + rows)
                inner[c, k, :, lanes] = jnp.where(odd, low, high)
                outer[c, k, :, lanes] = jnp.where(odd, high, low)


def main_kernel(offs, vids, got, absorb_part, emit_part, w, main, image, shifted):
    views, channels, rows, cols = w.shape
    slabs = main.shape[1]
    tiles = cols // LANES
    bands = rows // 8
    edge = jnp.zeros((4, LANES), jnp.float32)
    moves = [[offs[k, vids[v]] for k in range(slabs)] for v in range(views)]
    for t in range(tiles):
        lanes = pl.ds(t * LANES, LANES)
        for v in range(views):
            for b in range(bands):
                for c in range(channels):
                    image[v, c, 8 * b : 8 * b + 8, lanes] = got[v * bands + b, 2 + c, t]
        for v in range(views):
            grads = pixel_grads(got, absorb_part, emit_part, w, v, t, bands, slabs)
            for k, parts in grads:
                for c in range(channels):
                    shifted[v, k, c, t, 4:8, :] = edge
                    shifted[v, k, c, t, 8 : 8 + rows, :] = parts[c]
                    shifted[v, k, c, t, 8 + rows : 12 + rows, :] = edge
        for k in range(slabs):
            for c in range(channels):
                main[c, k, :, lanes] = sum(
                    shifted[v, k, c, t, pl.ds(8 + moves[v][k], rows), :] for v in range(views)
                )


def join_kernel(strip, main, inner, outer, out):
    rows = main.shape[2]
    odd = lax.rem(strip[0], 2) == 1
    near, far = inner[...], outer[...]
    out[:, :, 0:4, :] = main[:, :, 0:4, :] + jnp.where(odd, near, far)
    out[:, :, 4 : rows - 4, :] = main[:, :, 4 : rows - 4, :]
    out[:, :, rows - 4 :, :] = main[:, :, rows - 4 :, :] + jnp.where(odd, far, near)


def off_chip(x):
    return pltpu.with_memory_space_constraint(x, pltpu.HBM)


def on_chip(x):
    return pltpu.with_memory_space_constraint(x, pltpu.VMEM)


def on_device(volume, offsets, view_ids, weights):
    channels, slabs, rows, cols = volume.shape
    views = weights.shape[0]
    count = lax.axis_size("depth")
    strips = lax.axis_size("lat")
    tiles, bands = cols // LANES, rows // 8
    depth_total = slabs * count
    size = views * bands
    near = [[size * g + i for i in range(size)] for g in range(count // size)]
    near = [row[size // 2 :] + row[: size // 2] if g >= 2 else row for g, row in enumerate(near)]
    pairs = [(i, i ^ 1) for i in range(strips)]
    links = [(i, ((i + 1) ^ 1) - 1) for i in range(1, strips - 1)]
    f32 = lambda *shape: jax.ShapeDtypeStruct(shape, jnp.float32)
    kept = lambda *shape: pltpu.VMEM(shape, jnp.float32)
    table, view_ids = off_chip(offsets.T), off_chip(view_ids)
    place = lax.axis_index("depth").reshape(1).astype(jnp.int32)
    w = on_chip(weights)

    def swap(x, groups):
        return lax.all_to_all(x, "depth", 0, 0, tiled=True, axis_index_groups=groups)

    strip = lax.axis_index("lat").reshape(1).astype(jnp.int32)
    odd = (strip & 1) == 1
    first, last = volume[:, :, :HALO], volume[:, :, rows - HALO :]
    outer = lax.ppermute(jnp.where(odd, last, first), "lat", links)
    inner = lax.ppermute(jnp.where(odd, first, last), "lat", pairs)
    own = pl.pallas_call(
        fill_kernel,
        out_shape=kept(channels, slabs, tiles, rows + 16, LANES),
        in_specs=[VMEM],
        out_specs=VMEM,
        compiler_params=LIMIT,
        name="fill",
    )(on_chip(volume))
    agg, _, absorb_part, emit_part = pl.pallas_call(
        lambda *refs: slab_kernel(depth_total, *refs),
        out_shape=(
            kept(size, 4, tiles, 8, LANES),
            kept(channels, slabs, tiles, rows + 16, LANES),
            kept(views, slabs, tiles, rows, LANES),
            kept(views, slabs, tiles, rows, LANES),
        ),
        in_specs=[SMEM, SMEM, SMEM, SMEM, VMEM, VMEM, VMEM, VMEM],
        out_specs=(VMEM, VMEM, VMEM, VMEM),
        input_output_aliases={6: 1},
        compiler_params=LIMIT,
        name="slab",
    )(table, view_ids, strip, place, on_chip(inner), on_chip(outer), on_chip(own), w)
    agg = on_chip(swap(agg, near))
    grouped = pl.pallas_call(
        group_kernel,
        out_shape=kept(4, tiles, 8, LANES),
        in_specs=[SMEM, VMEM],
        out_specs=VMEM,
        compiler_params=LIMIT,
        name="group",
    )(place, agg)
    parts = {0: grouped}
    for j in (2, 3, 1):
        hops = [(a, b) for g, row in enumerate(near) for a, b in zip(row, near[g ^ j])]
        parts[j] = lax.ppermute(grouped, "depth", hops)
    parts = [on_chip(parts[j]) for j in range(count // size)]
    sent = pl.pallas_call(
        scan_kernel,
        out_shape=kept(size, 6, tiles, 8, LANES),
        in_specs=[SMEM] + [VMEM] * (2 + count // size),
        out_specs=VMEM,
        compiler_params=LIMIT,
        name="scan",
    )(place, agg, *parts, w)
    got = on_chip(swap(sent, near))

    to_inner, to_outer = pl.pallas_call(
        edge_kernel,
        out_shape=(
            kept(channels, slabs, HALO, cols),
            kept(channels, slabs, HALO, cols),
        ),
        in_specs=[SMEM, SMEM, SMEM, VMEM, VMEM, VMEM, VMEM],
        out_specs=(VMEM, VMEM),
        scratch_shapes=[
            pltpu.VMEM((views, slabs, channels, tiles, rows + 16, LANES), jnp.float32)
        ],
        compiler_params=LIMIT,
        name="edge",
    )(table, view_ids, strip, got, on_chip(absorb_part), on_chip(emit_part), w)
    from_outer = lax.ppermute(to_outer, "lat", links)
    from_inner = lax.ppermute(to_inner, "lat", pairs)
    main, image_out = pl.pallas_call(
        main_kernel,
        out_shape=(kept(channels, slabs, rows, cols), f32(views, channels, rows, cols)),
        in_specs=[SMEM, SMEM, VMEM, VMEM, VMEM, VMEM],
        out_specs=(VMEM, VMEM),
        scratch_shapes=[
            pltpu.VMEM((views, slabs, channels, tiles, rows + 16, LANES), jnp.float32)
        ],
        compiler_params=LIMIT,
        name="main",
    )(table, view_ids, got, on_chip(absorb_part), on_chip(emit_part), w)
    grad_out = pl.pallas_call(
        join_kernel,
        out_shape=f32(channels, slabs, rows, cols),
        in_specs=[SMEM, VMEM, VMEM, VMEM],
        out_specs=VMEM,
        compiler_params=LIMIT,
        name="join",
    )(strip, on_chip(main), on_chip(from_inner), on_chip(from_outer))
    return (image_out, grad_out)


def solution(mesh):
    in_specs = (P(None, "depth", "lat", None), P(None, "depth"), P(), P(None, None, "lat", None))
    out_specs = (P(None, None, "lat", None), P(None, "depth", "lat", None))
    return jax.shard_map(
        on_device, mesh=mesh, in_specs=in_specs, out_specs=out_specs, check_vma=False
    )
```
